256 devices in a mesh: lat: 4 (over y), col: 64 (over z, x, core).
Axes of the slice: x: 4, y: 4, z: 8, core: 2. Of those that a mesh axis runs over, the one named last changes fastest.
Arguments:
- control: float32 [128, 16384], P('lat', 'col'), may hold values from -6 to 6
- perturbations: float32 [128, 16384, 128], P('lat', 'col'), may hold values from -6 to 6
- zonal_flow: float32 [128, 16384], P('lat', 'col'), may hold values from -0.25 to 0.25
- meridional_flow: float32 [128, 16384], P('lat', 'col'), may hold values from -0.25 to 0.25
- diffusivity: float32 [128, 16384], P('lat', 'col'), may hold values from 0.03 to 0.12
- send_cell: int32 [4, 64, 64, 128], P('lat', 'col'), may hold values from 0 to 8191
- send_station: int32 [4, 64, 64, 128], P('lat', 'col'), may hold values from 0 to 255
- send_weight: float32 [4, 64, 64, 128], P('lat', 'col'), may hold values from 0.2 to 1
- send_count: int32 [4, 64, 64], P('lat', 'col'), may hold values from 32 to 128, as said below
- obs_value: float32 [2, 65536], P(None, ('lat', 'col')), may hold values from -24 to 24
- obs_error: float32 [2, 65536], P(None, ('lat', 'col')), may hold values from 1.3 to 64, as said below
Outputs:
- analysis: float32 [128, 16384, 128], P('lat', 'col')
- obs_analysis: float32 [2, 65536, 128], P(None, ('lat', 'col'))
The draws below stay inside these ranges and needn't reach their ends.
Inputs may be any that keep to these rules, and one draw needn't show every extreme that they name: send_count[l, e, d] counts the live leading slots that device e of latitude group l fills for device d of its group; in every group one device d receives all 128 slots from every source. obs_error is positive.
All inputs are finite; a program needn't handle non-finite values.
Results may differ from the reference program's by a relative error of at most 0.0003.
Values sent between devices are 32-bit elements; how exact they have to be, the bound alone decides.
No kernel may reach another device: no remote copies, remote signals or barrier semaphores. Data moves between devices by JAX's collectives and lax.ppermute only.
A program may use at most 128 MiB of HBM per device.

```python
import math
import jax
import jax.numpy as jnp
from jax import lax

M = 128
CX = 32
CY = 256
OBS_DEV = 256
CAP = 128
STEPS = 2
NX = 128
NY = 16384
OBS = 65536
N_LAT = 4
N_COL = 64


def draw_send_count(key, part):
    key_base, key_busy = jax.random.split(key)
    counts = jax.random.randint(key_base, (N_LAT, N_COL, N_COL), CAP // 4, CAP + 1)
    busiest = jax.random.randint(key_busy, (N_LAT, 1, 1), 0, N_COL)
    column = jnp.arange(N_COL, dtype=jnp.int32)[None, None, :]
    return jnp.where(column == busiest, CAP, counts).astype(jnp.int32)


def draw_obs_error(key, part):
    placing = jnp.arange(OBS, dtype=jnp.float32) / OBS
    spread = jnp.exp(jax.random.uniform(key, (STEPS, OBS), jnp.float32, jnp.log(4.0), jnp.log(64.0)))
    return (spread * jnp.exp(-jnp.log(3.0) * placing)[None, :]).astype(jnp.float32)


def with_ends(entries, key, smallest, largest):
    place = [jax.random.randint(jax.random.fold_in(key, axis), (), 0, length) for axis, length in enumerate(entries.shape)]
    main_axis = entries.shape.index(max(entries.shape))
    beside = place[:main_axis] + [(place[main_axis] + 1) % entries.shape[main_axis]] + place[main_axis + 1:]
    return entries.at[tuple(place)].set(smallest).at[tuple(beside)].set(largest)


def block_levels(stream_key, dims, pieces, low, largest):
    loudness, own = 1.0, jax.random.fold_in(stream_key, 6)
    for position, parts in pieces:
        heights = jnp.exp(jax.random.uniform(jax.random.fold_in(own, position), (parts,), jnp.float32, low / len(pieces), largest / len(pieces)))
        loudness = loudness * jnp.repeat(heights, dims[position] // parts).reshape([-1 if axis == position else 1 for axis in range(len(dims))])
    return loudness


def bell_draw(key, dims, scale, limit, cuts=(), kind=jnp.bfloat16):
    values = scale * jax.random.normal(key, dims, jnp.float32)
    if cuts:
        values = values * block_levels(key, dims, cuts, -0.22, 0.18)
    return jnp.clip(values, -limit, limit).astype(kind)


def setup_inputs(seed: int = 0) -> dict:
    streams_of = jax.random.split(jax.random.key(seed), 12)
    return {
        "control": bell_draw(streams_of[0], (NX, NY), 1.0, 6.0, ((0, 4), (1, 64)), jnp.float32),
        "perturbations": bell_draw(streams_of[1], (NX, NY, M), 1.0, 6.0, ((0, 4), (1, 64)), jnp.float32),
        "zonal_flow": jnp.clip(jax.random.uniform(streams_of[2], (NX, NY), jnp.float32, -0.25, 0.25) * block_levels(streams_of[2], (NX, NY), ((0, 4), (1, 64)), -0.4, 0.0), -0.25, 0.25),
        "meridional_flow": jnp.clip(jax.random.uniform(streams_of[3], (NX, NY), jnp.float32, -0.25, 0.25) * block_levels(streams_of[3], (NX, NY), ((0, 4), (1, 64)), -0.4, 0.0), -0.25, 0.25),
        "diffusivity": jnp.clip(jnp.exp(math.log(0.12) - 1.3862944 * jax.random.uniform(streams_of[4], (NX, NY), jnp.float32) ** block_levels(streams_of[4], (NX, NY), ((0, 4), (1, 64)), -0.2, 0.2)), 0.03, 0.12),
        "send_cell": with_ends(jax.random.randint(streams_of[5], (N_LAT, N_COL, N_COL, CAP), 0, CX * CY), jax.random.fold_in(streams_of[5], 1), 0, (CX * CY) - 1).astype(jnp.int32),
        "send_station": with_ends(jax.random.randint(streams_of[6], (N_LAT, N_COL, N_COL, CAP), 0, OBS_DEV), jax.random.fold_in(streams_of[6], 1), 0, OBS_DEV - 1).astype(jnp.int32),
        "send_weight": jnp.clip(0.2 + 0.8 * jax.random.uniform(streams_of[7], (N_LAT, N_COL, N_COL, CAP), jnp.float32) ** block_levels(streams_of[7], (N_LAT, N_COL, N_COL, CAP), ((0, 4), (1, 64)), -0.2, 0.2), 0.2, 1.0),
        "send_count": draw_send_count(jax.random.fold_in(streams_of[11], 71), 0),
        "obs_value": bell_draw(streams_of[9], (STEPS, OBS), 4.0, 24.0, ((1, 256),), jnp.float32),
        "obs_error": draw_obs_error(jax.random.fold_in(streams_of[11], 71), 0),
    }


exact_mode = lax.Precision.HIGHEST

def upwind_rates(zonal, meridional, diffusion):
    east_rate = diffusion + jnp.maximum(-zonal, 0.0)
    west_rate = diffusion + jnp.maximum(zonal, 0.0)
    north_rate = diffusion + jnp.maximum(-meridional, 0.0)
    south_rate = diffusion + jnp.maximum(meridional, 0.0)
    return (east_rate[..., None], west_rate[..., None], north_rate[..., None], south_rate[..., None])

def advance(padded, coeffs):
    centre = padded[1:-1, 1:-1]
    result = centre + coeffs[0] * (padded[2:, 1:-1] - centre)
    result = result + coeffs[1] * (padded[:-2, 1:-1] - centre)
    result = result + coeffs[2] * (padded[1:-1, 2:] - centre)
    return result + coeffs[3] * (padded[1:-1, :-2] - centre)

def reference(control, perturbations, zonal_flow, meridional_flow, diffusivity, send_cell, send_station, send_weight, send_count, obs_value, obs_error):
    members = perturbations + control[:, :, None]
    coeffs = upwind_rates(zonal_flow, meridional_flow, diffusivity)
    prior_ensemble_matrix = []
    current_model_vector = members
    for time_index in range(STEPS):
        padded = jnp.pad(current_model_vector, ((1, 1), (1, 1), (0, 0)))
        current_model_vector = advance(padded, coeffs)
        prior_ensemble_matrix.append(current_model_vector)
    live_slot = jnp.arange(CAP, dtype=jnp.int32)[None, None, None, :] < send_count[..., None]
    factors = jnp.where(live_slot, send_weight, 0.0)
    destination = jnp.arange(N_COL, dtype=jnp.int32)[:, None]
    zero_index = jnp.zeros((), jnp.int32)

    def measure_operator(field):

        def visit(totals, source_id):
            lat_group = source_id // N_COL
            sender = source_id % N_COL
            device_block = lax.dynamic_slice(field, (lat_group * CX, sender * CY, zero_index), (CX, CY, M)).reshape(CX * CY, M)
            cell_ids = send_cell[lat_group, sender].reshape(-1)
            picked = device_block[cell_ids] * factors[lat_group, sender].reshape(-1)[:, None]
            target = ((lat_group * N_COL + destination) * OBS_DEV + send_station[lat_group, sender]).reshape(-1)
            return (totals.at[target].add(picked), None)
        result, unused = lax.scan(visit, jnp.zeros((OBS, M), jnp.float32), jnp.arange(N_LAT * N_COL, dtype=jnp.int32))
        return result
    root_scale = math.sqrt(M - 1.0)
    gram = jnp.eye(M, dtype=jnp.float32)
    push = jnp.zeros((M,), jnp.float32)
    means = []
    spreads = []
    for time_index in range(STEPS):
        measurement_vector = measure_operator(prior_ensemble_matrix[time_index])
        obs_mean = lax.optimization_barrier(jnp.mean(measurement_vector, axis=1))
        spread = measurement_vector - obs_mean[:, None]
        scaled = spread / (obs_error[time_index][:, None] * root_scale)
        innovation = (obs_value[time_index] - obs_mean) / obs_error[time_index]
        gram = gram + jnp.dot(scaled.T, scaled, precision=exact_mode)
        push = push + jnp.dot(innovation, scaled, precision=exact_mode)
        means.append(obs_mean)
        spreads.append(spread)
    factor = jnp.linalg.cholesky(gram)
    identity = jnp.eye(M, dtype=jnp.float32)
    inverse = lax.linalg.triangular_solve(factor, identity, left_side=True, lower=True)
    offset = jnp.dot(inverse.T, jnp.dot(inverse, push, precision=exact_mode), precision=exact_mode) / root_scale
    weights = inverse.T + offset[:, None]
    final_model_vector = prior_ensemble_matrix[-1]
    state_mean = lax.optimization_barrier(jnp.mean(final_model_vector, axis=2, keepdims=True))
    departures = (final_model_vector - state_mean).reshape(-1, M)
    analysis = state_mean + jnp.dot(departures, weights, precision=exact_mode).reshape(final_model_vector.shape)
    obs_analysis = jnp.stack([means[k][:, None] + jnp.dot(spreads[k], weights, precision=exact_mode) for k in range(STEPS)])
    return (analysis, obs_analysis)
```

```python
import functools
import math

import jax
import jax.numpy as jnp
from jax import lax
from jax.experimental import pallas as pl
from jax.experimental.pallas import tpu as pltpu
from jax.sharding import Mesh
from jax.sharding import PartitionSpec as P

exact_mode = lax.Precision.HIGHEST
COL = ("z", "x", "core")
UNROLL = 16


def shift(value, axis, step):
    count = lax.axis_size(axis)
    return lax.ppermute(value, axis, [(i, (i + step) % count) for i in range(count)])


def with_halo(block, sides, width):
    for axis, dim in sides:
        names = axis if isinstance(axis, tuple) else (axis,)
        count = math.prod(lax.axis_size(name) for name in names)
        forward = [(i, i + 1) for i in range(count - 1)]
        backward = [(target, source) for source, target in forward]
        low = lax.ppermute(
            lax.slice_in_dim(block, block.shape[dim] - width, None, axis=dim), axis, forward
        )
        high = lax.ppermute(lax.slice_in_dim(block, 0, width, axis=dim), axis, backward)
        block = jnp.concatenate([low, block, high], axis=dim)
    return block


def upwind_rates(zonal, meridional, diffusion):
    east_rate = diffusion + jnp.maximum(-zonal, 0.0)
    west_rate = diffusion + jnp.maximum(zonal, 0.0)
    north_rate = diffusion + jnp.maximum(-meridional, 0.0)
    south_rate = diffusion + jnp.maximum(meridional, 0.0)
    return (
        east_rate[..., None],
        west_rate[..., None],
        north_rate[..., None],
        south_rate[..., None],
    )


def advance(padded, coeffs):
    centre = padded[1:-1, 1:-1]
    result = centre + coeffs[0] * (padded[2:, 1:-1] - centre)
    result = result + coeffs[1] * (padded[:-2, 1:-1] - centre)
    result = result + coeffs[2] * (padded[1:-1, 2:] - centre)
    return result + coeffs[3] * (padded[1:-1, :-2] - centre)


def bin_kernel(adds, size_z, size_x, place, cell, weight, count, station, first, second, *rest):
    if adds:
        before_a, before_b, out_a, out_b, picked = rest
    else:
        out_a, out_b, picked = rest
    step = pl.program_id(0)
    receiver = ((place[0] + step // size_x) % size_z) * size_x + (place[1] + step % size_x) % size_x
    owned = out_a.shape[2] + out_b.shape[2]
    owned = owned // 2
    cut = out_a.shape[2] - owned

    @pl.when(step == 0)
    def _():
        picked[...] = jnp.zeros_like(picked)

    def pick(group, carry):
        for j in range(UNROLL):
            row = cell[receiver, group * UNROLL + j]
            factor = weight[receiver, group * UNROLL + j]
            tile, line = group * (UNROLL // 8) + j // 8, j % 8
            picked[0, tile, line : line + 1, :] = first[pl.ds(row, 1), :] * factor
            picked[1, tile, line : line + 1, :] = second[pl.ds(row, 1), :] * factor
        return carry

    lax.fori_loop(0, (count[receiver] + UNROLL - 1) // UNROLL, pick, 0)
    slots = station.shape[1]
    own = lax.broadcasted_iota(jnp.int32, (owned, slots), 0)
    hot = jnp.where(station[pl.ds(receiver, 1), :] == own, 1.0, 0.0).astype(jnp.bfloat16)
    value = jnp.concatenate(
        [picked[0].reshape(slots, -1), picked[1].reshape(slots, -1)], axis=1
    )
    high = value.astype(jnp.bfloat16)
    low = (value - high.astype(jnp.float32)).astype(jnp.bfloat16)
    total = jnp.dot(
        jnp.concatenate([hot, hot], axis=1),
        jnp.concatenate([high, low], axis=0),
        preferred_element_type=jnp.float32,
    )
    width = first.shape[1]
    one, two = total[:, :width], total[:, width:]
    if adds:
        out_a[0, 0, :owned, :] = before_a[0, 0, :owned, :] + one
        out_a[0, 0, owned:, :] = before_a[0, 0, owned:, :] + two[:cut]
        out_b[0, 0] = before_b[0, 0] + two[cut:]
    else:
        out_a[0, 0, :owned, :] = one
        out_a[0, 0, owned:, :] = two[:cut]
        out_b[0, 0] = two[cut:]


def bin_rows(place, cell, weight, count, station, first, second, owned, before=None):
    size_z, size_x = lax.axis_size("z"), lax.axis_size("x")
    members = first.shape[1]
    rows_a = owned + owned // 8
    rows_b = 2 * owned - rows_a
    scalar = pl.BlockSpec(memory_space=pltpu.SMEM)
    whole = pl.BlockSpec(memory_space=pltpu.VMEM)
    blocks = [
        pl.BlockSpec((1, 1, rows, members), lambda k: (k // size_x, k % size_x, 0, 0))
        for rows in (rows_a, rows_b)
    ]
    return pl.pallas_call(
        functools.partial(bin_kernel, before is not None, size_z, size_x),
        grid=(size_z * size_x,),
        in_specs=[scalar] * 4 + [whole] * 3 + (blocks if before is not None else []),
        out_specs=blocks,
        out_shape=[
            jax.ShapeDtypeStruct((size_z, size_x, rows, members), jnp.float32)
            for rows in (rows_a, rows_b)
        ],
        scratch_shapes=[pltpu.VMEM((2, cell.shape[1] // 8, 8, members), jnp.float32)],
        compiler_params=pltpu.CompilerParams(vmem_limit_bytes=48 * 2**20),
        cost_estimate=pl.CostEstimate(flops=10**9, bytes_accessed=30 * 2**20, transcendentals=0),
    )(place, cell, weight, count, station, first, second, *(before or ()))


def ring_reduce(blocks, axis):
    count = len(blocks)
    half = count // 2
    cut = blocks[half].shape[-2] // 2
    up = shift(blocks[half][..., :cut, :], axis, 1)
    down = shift(blocks[half][..., cut:, :], axis, -1)
    ahead, behind = blocks[half - 1], blocks[count - half + 1]
    up = jnp.concatenate([ahead[..., :cut, :] + up, ahead[..., cut:, :]], axis=-2)
    down = jnp.concatenate([behind[..., :cut, :], behind[..., cut:, :] + down], axis=-2)
    for k in range(half - 1, 0, -1):
        up = shift(up, axis, 1)
        down = shift(down, axis, -1)
        if k > 1:
            up = blocks[k - 1] + up
            down = blocks[count - k + 1] + down
    return blocks[0] + up + down


def reduce_to_owner(block_a, block_b):
    size_z, size_x = block_a.shape[:2]
    part_a = ring_reduce([block_a[:, k] for k in range(size_x)], "x")
    part_b = ring_reduce([block_b[k] for k in range(size_z)], "z")
    part_a = ring_reduce([part_a[k] for k in range(size_z)], "z")
    part_b = ring_reduce([part_b[k] for k in range(size_x)], "x")
    return jnp.concatenate([part_a, part_b], axis=0)


def spread_sum(value, axis):
    count = lax.axis_size(axis)
    copies = jnp.broadcast_to(value[None], (count,) + value.shape)
    return jnp.sum(lax.all_to_all(copies, axis, split_axis=0, concat_axis=0, tiled=True), axis=0)


def sum_everywhere(value):
    core = lax.axis_index("core")
    rows = value.shape[0] // 2
    value = value + shift(value, "core", 1)
    part = lax.dynamic_slice_in_dim(value, core * rows, rows, 0)
    for axis in ("x", "lat", "z"):
        part = spread_sum(part, axis)
    other = shift(part, "core", 1)
    return jnp.where(
        core == 0, jnp.concatenate([part, other]), jnp.concatenate([other, part])
    )


def on_device(
    control,
    perturbations,
    zonal_flow,
    meridional_flow,
    diffusivity,
    send_cell,
    send_station,
    send_weight,
    send_count,
    obs_value,
    obs_error,
):
    members = perturbations + control[:, :, None]
    member_count = perturbations.shape[2]
    step_total, owned_count = obs_value.shape
    slots = send_cell.shape[3]
    size_z, size_x, size_c = (lax.axis_size(name) for name in COL)
    core = lax.axis_index("core")
    place = jnp.stack([lax.axis_index("z"), lax.axis_index("x")]).astype(jnp.int32)

    live = lax.broadcasted_iota(jnp.int32, send_cell.shape[2:], 1) < send_count[0, 0][:, None]
    station_live = jnp.where(live, send_station[0, 0], -1)
    whole_tables = jnp.concatenate(
        [
            send_cell[0, 0],
            station_live,
            jnp.broadcast_to(send_count[0, 0][:, None], (send_cell.shape[2], slots)),
        ],
        axis=1,
    ).reshape(size_z * size_x, size_c, 3 * slots)
    whole_weights = send_weight[0, 0].reshape(size_z * size_x, size_c, slots)
    index_own = lax.dynamic_index_in_dim(whole_tables, core, 1, keepdims=False)
    index_pair = shift(
        lax.dynamic_index_in_dim(whole_tables, 1 - core, 1, keepdims=False), "core", 1
    )
    weight_own = lax.dynamic_index_in_dim(whole_weights, core, 1, keepdims=False)
    weight_pair = shift(
        lax.dynamic_index_in_dim(whole_weights, 1 - core, 1, keepdims=False), "core", 1
    )

    inner_rates = upwind_rates(zonal_flow, meridional_flow, diffusivity)
    states = []
    current = members
    for _ in range(step_total):
        current = advance(with_halo(current, (("lat", 0), (COL, 1)), 1), inner_rates)
        states.append(current)
    flat = [state.reshape(-1, member_count) for state in states]
    paired = [shift(state, "core", 1) for state in flat]

    def tables(index, weight):
        return (
            place,
            index[:, :slots],
            weight,
            index[:, 2 * slots],
            index[:, slots : 2 * slots],
        )

    blocks = bin_rows(*tables(index_own, weight_own), *flat, owned_count)
    blocks = bin_rows(*tables(index_pair, weight_pair), *paired, owned_count, tuple(blocks))
    observed = reduce_to_owner(*blocks).reshape(step_total, owned_count, member_count)

    root_scale = math.sqrt(member_count - 1.0)
    obs_mean = jnp.mean(observed, axis=2)
    spread = observed - obs_mean[:, :, None]
    scaled = (spread / (obs_error[:, :, None] * root_scale)).reshape(-1, member_count)
    innovation = ((obs_value - obs_mean) / obs_error).reshape(-1)
    products = jnp.dot(
        jnp.concatenate(
            [scaled, innovation[:, None], jnp.zeros((scaled.shape[0], 15), jnp.float32)], axis=1
        ).T,
        scaled,
        precision=exact_mode,
    )
    products = sum_everywhere(products)
    total_gram, total_push = products[:member_count], products[member_count]

    identity = jnp.eye(member_count, dtype=jnp.float32)
    factor = jnp.linalg.cholesky(identity + total_gram)
    inverse = lax.linalg.triangular_solve(factor, identity, left_side=True, lower=True)
    offset = (
        jnp.dot(inverse.T, jnp.dot(inverse, total_push, precision=exact_mode), precision=exact_mode)
        / root_scale
    )
    weights = inverse.T + offset[:, None]
    final = flat[-1]
    state_mean = jnp.mean(final, axis=1, keepdims=True)
    analysis = state_mean + jnp.dot(final - state_mean, weights, precision=exact_mode)
    obs_analysis = obs_mean[:, :, None] + jnp.dot(spread, weights, precision=exact_mode)
    return (analysis.reshape(perturbations.shape), obs_analysis)


def solution(mesh):
    sizes = (mesh.shape["lat"], mesh.shape["col"] // 8, 4, 2)
    fine = Mesh(mesh.devices.reshape(sizes), ("lat",) + COL)
    grid = P("lat", COL)
    return jax.shard_map(
        on_device,
        mesh=fine,
        in_specs=(
            grid,
            P("lat", COL, None),
            grid,
            grid,
            grid,
            P("lat", COL, None, None),
            P("lat", COL, None, None),
            P("lat", COL, None, None),
            P("lat", COL, None),
            P(None, ("lat",) + COL),
            P(None, ("lat",) + COL),
        ),
        out_specs=(P("lat", COL, None), P(None, ("lat",) + COL, None)),
        check_vma=False,
    )
```

```python
import functools
import math

import jax
import jax.numpy as jnp
from jax import lax
from jax.experimental import pallas as pl
from jax.experimental.pallas import tpu as pltpu
from jax.sharding import Mesh
from jax.sharding import PartitionSpec as P

exact_mode = lax.Precision.HIGHEST
COL = ("z", "x", "core")
UNROLL = 16


def shift(value, axis, step):
    count = lax.axis_size(axis)
    return lax.ppermute(value, axis, [(i, (i + step) % count) for i in range(count)])


def edges(block):
    sides = []
    for axis, dim in (("lat", 0), (COL, 1)):
        names = axis if isinstance(axis, tuple) else (axis,)
        count = math.prod(lax.axis_size(name) for name in names)
        forward = [(i, i + 1) for i in range(count - 1)]
        backward = [(target, source) for source, target in forward]
        last = lax.slice_in_dim(block, block.shape[dim] - 1, None, axis=dim)
        first = lax.slice_in_dim(block, 0, 1, axis=dim)
        sides.append(lax.ppermute(last, axis, forward))
        sides.append(lax.ppermute(first, axis, backward))
    return sides


def advance_kernel(adds, rates, block, above, below, left, right, out, padded, turned):
    rows, cells, members = block.shape
    groups, lanes = rates.shape[0], rates.shape[1]
    per_group = rows // groups
    for group in range(groups):
        turned[group] = jnp.transpose(rates[group])
    padded[0, 8 : 8 + cells, :] = above[0]
    padded[rows + 1, 8 : 8 + cells, :] = below[0]

    def rate(i, kind):
        lane = (i % per_group) * (lanes // per_group) + kind
        index = jnp.full((cells, members), lane, jnp.int32)
        return jnp.take_along_axis(turned[i // per_group], index, axis=1)

    def fill(i, carry):
        value = block[i]
        padded[i + 1, 8 : 8 + cells, :] = value + rate(i, 4) if adds else value
        padded[i + 1, 7:8, :] = left[i]
        padded[i + 1, 8 + cells : 9 + cells, :] = right[i]
        return carry

    lax.fori_loop(0, rows, fill, 0)

    def row(i, carry):
        centre = padded[i + 1, 8 : 8 + cells, :]
        result = centre + rate(i, 0) * (padded[i + 2, 8 : 8 + cells, :] - centre)
        result = result + rate(i, 1) * (padded[i, 8 : 8 + cells, :] - centre)
        result = result + rate(i, 2) * (padded[i + 1, 9 : 9 + cells, :] - centre)
        out[i] = result + rate(i, 3) * (padded[i + 1, 7 : 7 + cells, :] - centre)
        return carry

    lax.fori_loop(0, rows, row, 0)


def advance(adds, rates, block, sides):
    rows, cells, members = block.shape
    whole = pl.BlockSpec(memory_space=pltpu.VMEM)
    return pl.pallas_call(
        functools.partial(advance_kernel, adds),
        in_specs=[whole] * 6,
        out_specs=whole,
        out_shape=pltpu.VMEM(block.shape, jnp.float32),
        scratch_shapes=[
            pltpu.VMEM((rows + 2, cells + 16, members), jnp.float32),
            pltpu.VMEM((rates.shape[0], cells, rates.shape[1]), jnp.float32),
        ],
        compiler_params=pltpu.CompilerParams(vmem_limit_bytes=24 * 2**20),
        cost_estimate=pl.CostEstimate(
            flops=12 * block.size, bytes_accessed=8 * block.size, transcendentals=0
        ),
    )(rates, block, *sides)


def bin_kernel(
    size_z, size_x, owned, place, cell, weight, count, station, *rest
):
    states, (out_a, out_b, picked) = rest[:4], rest[4:]
    width = out_a.shape[3]
    cut = out_a.shape[2] - owned
    receivers, slots = size_z * size_x, station.shape[1]
    picked[...] = jnp.zeros_like(picked)
    own = lax.broadcasted_iota(jnp.int32, (owned, slots), 0)

    def one(step, carry):
        ahead_z, ahead_x = step // size_x, step % size_x
        receiver = ((place[0] + ahead_z) % size_z) * size_x + (place[1] + ahead_x) % size_x
        hots = []
        for e in range(2):
            first, second = states[2 * e], states[2 * e + 1]
            entry = e * receivers + receiver

            def pick(group, inner):
                for j in range(UNROLL):
                    slot = entry * slots + group * UNROLL + j
                    row, factor = cell[slot], weight[slot]
                    tile, line = group * (UNROLL // 8) + j // 8, j % 8
                    picked[e, 0, tile, line : line + 1, :] = first[pl.ds(row, 1), :] * factor
                    picked[e, 1, tile, line : line + 1, :] = second[pl.ds(row, 1), :] * factor
                return inner

            lax.fori_loop(0, (count[entry] + UNROLL - 1) // UNROLL, pick, 0)
            hit = station[pl.ds(entry, 1), :] == own
            hots.append(jnp.where(hit, 1.0, 0.0).astype(jnp.bfloat16))
        value = jnp.concatenate(
            [
                jnp.concatenate([picked[e, k].reshape(slots, width) for k in range(2)], axis=1)
                for e in range(2)
            ],
            axis=0,
        )
        high = value.astype(jnp.bfloat16)
        low = (value - high.astype(jnp.float32)).astype(jnp.bfloat16)
        total = jnp.dot(
            jnp.concatenate(hots + hots, axis=1),
            jnp.concatenate([high, low], axis=0),
            preferred_element_type=jnp.float32,
        )
        out_a[ahead_x, ahead_z, :owned, :] = total[:, :width]
        out_a[ahead_x, ahead_z, owned:, :] = total[:cut, width:]
        out_b[ahead_z, ahead_x] = total[cut:, width:]
        return carry

    lax.fori_loop(0, receivers, one, 0)


def bin_rows(place, cell, weight, count, station, states, owned):
    size_z, size_x = lax.axis_size("z"), lax.axis_size("x")
    members, slots = states[0].shape[1], station.shape[1]
    rows_a = owned + owned // 8
    rows_b = 2 * owned - rows_a
    scalar = pl.BlockSpec(memory_space=pltpu.SMEM)
    whole = pl.BlockSpec(memory_space=pltpu.VMEM)
    return pl.pallas_call(
        functools.partial(bin_kernel, size_z, size_x, owned),
        in_specs=[scalar] * 4 + [whole] * 5,
        out_specs=[whole] * 2,
        out_shape=[
            pltpu.VMEM((size_x, size_z, rows_a, members), jnp.float32),
            pltpu.VMEM((size_z, size_x, rows_b, members), jnp.float32),
        ],
        scratch_shapes=[pltpu.VMEM((2, 2, slots // 8, 8, members), jnp.float32)],
        compiler_params=pltpu.CompilerParams(vmem_limit_bytes=48 * 2**20),
        cost_estimate=pl.CostEstimate(flops=10**9, bytes_accessed=30 * 2**20, transcendentals=0),
    )(place, cell, weight, count, station, *states)


def factor_kernel(root_scale, products, high, low):
    size = products.shape[1]
    lane = lax.broadcasted_iota(jnp.int32, (size, size), 1)
    line = lax.broadcasted_iota(jnp.int32, (size, size), 0)
    eye = jnp.where(lane == line, 1.0, 0.0)
    left, right = products[:size, :] + eye, eye
    width = 4
    done_left, done_right = [], []
    for start in range(0, size, width):
        top = start % 8
        columns = [
            jnp.broadcast_to(left[:, start + a : start + a + 1], left.shape) for a in range(width)
        ]
        pivots = [[columns[b][top + a : top + a + 1, :] for b in range(width)] for a in range(width)]
        upper = [[None] * width for _ in range(width)]
        inverse = []
        for a in range(width):
            lower = []
            for k in range(a):
                value = pivots[a][k]
                for m in range(k):
                    value = value - lower[m] * upper[m][k]
                lower.append(value * inverse[k])
            for b in range(a, width):
                value = pivots[a][b]
                for m in range(a):
                    value = value - lower[m] * upper[m][b]
                upper[a][b] = value
            inverse.append(1.0 / upper[a][a])
        below = line[: left.shape[0]]
        multipliers = []
        for a in range(width):
            value = columns[a]
            for m in range(a):
                value = value - multipliers[m] * upper[m][a]
            value = value * inverse[a]
            multipliers.append(jnp.where(below > top + a, value, 0.0))
        rows_left, rows_right = [], []
        for a in range(width):
            row_left = left[top + a : top + a + 1, :]
            row_right = right[top + a : top + a + 1, :]
            for m in range(a):
                scale = multipliers[m][top + a : top + a + 1, :]
                row_left = row_left - scale * rows_left[m]
                row_right = row_right - scale * rows_right[m]
            rows_left.append(row_left)
            rows_right.append(row_right)
        for m in range(width):
            left = left - multipliers[m] * rows_left[m]
            right = right - multipliers[m] * rows_right[m]
        if top + width == 8:
            done_left.append(left[:8])
            done_right.append(right[:8])
            left, right = left[8:], right[8:]
    left = jnp.concatenate(done_left, axis=0)
    right = jnp.concatenate(done_right, axis=0)
    pivot = jnp.sum(jnp.where(lane == line, left, 0.0), axis=1, keepdims=True)
    inverse = right * lax.rsqrt(pivot)
    push = products[size : size + 1, :]
    pushed = jnp.sum(inverse * push, axis=1, keepdims=True)
    offset = jnp.sum(inverse * pushed, axis=0, keepdims=True) * (1.0 / root_scale)
    weights = inverse + offset
    top_half = weights.astype(jnp.bfloat16)
    high[...] = top_half
    low[...] = (weights - top_half.astype(jnp.float32)).astype(jnp.bfloat16)


def transposed_weights(products, root_scale):
    size = products.shape[1]
    whole = pl.BlockSpec(memory_space=pltpu.VMEM)
    return pl.pallas_call(
        functools.partial(factor_kernel, root_scale),
        in_specs=[whole],
        out_specs=[whole] * 2,
        out_shape=[jax.ShapeDtypeStruct((size, size), jnp.bfloat16)] * 2,
    )(products)


def analysis_kernel(high, low, state, out):
    value = state[...]
    mean = jnp.mean(value, axis=1, keepdims=True)
    departure = value - mean
    near = departure.astype(jnp.bfloat16)
    rest = (departure - near.astype(jnp.float32)).astype(jnp.bfloat16)

    def times(a, b):
        return lax.dot_general(
            a, b[...], (((1,), (1,)), ((), ())), preferred_element_type=jnp.float32
        )

    out[...] = mean + (times(near, high) + (times(rest, high) + times(near, low)))


def analyse(high, low, state):
    rows, members = state.shape
    size = min(rows, 1024)
    block = pl.BlockSpec((size, members), lambda k: (k, 0))
    whole = pl.BlockSpec(memory_space=pltpu.VMEM)
    return pl.pallas_call(
        analysis_kernel,
        grid=(rows // size,),
        in_specs=[whole, whole, block],
        out_specs=block,
        out_shape=jax.ShapeDtypeStruct(state.shape, jnp.float32),
    )(high, low, state)


def ring_reduce(blocks, axis):
    count = len(blocks)
    half = count // 2
    cut = blocks[half].shape[-2] // 2
    up = shift(blocks[half][..., :cut, :], axis, 1)
    down = shift(blocks[half][..., cut:, :], axis, -1)
    ahead, behind = blocks[half - 1], blocks[count - half + 1]
    up = jnp.concatenate([ahead[..., :cut, :] + up, ahead[..., cut:, :]], axis=-2)
    down = jnp.concatenate([behind[..., :cut, :], behind[..., cut:, :] + down], axis=-2)
    for k in range(half - 1, 0, -1):
        up = shift(up, axis, 1)
        down = shift(down, axis, -1)
        if k > 1:
            up = blocks[k - 1] + up
            down = blocks[count - k + 1] + down
    return blocks[0] + up + down


def reduce_to_owner(block_a, block_b):
    size_x, size_z = block_a.shape[:2]
    part_a = ring_reduce([block_a[k] for k in range(size_x)], "x")
    part_b = ring_reduce([block_b[k] for k in range(size_z)], "z")
    part_a = ring_reduce([part_a[k] for k in range(size_z)], "z")
    part_b = ring_reduce([part_b[k] for k in range(size_x)], "x")
    return jnp.concatenate([part_a, part_b], axis=0)


def spread_sum(value, axis):
    count = lax.axis_size(axis)
    copies = jnp.broadcast_to(value[None], (count,) + value.shape)
    return jnp.sum(lax.all_to_all(copies, axis, split_axis=0, concat_axis=0, tiled=True), axis=0)


def sum_everywhere(value):
    core = lax.axis_index("core")
    rows = value.shape[0] // 2
    value = value + shift(value, "core", 1)
    part = lax.dynamic_slice_in_dim(value, core * rows, rows, 0)
    for axis in ("x", "lat", "z"):
        part = spread_sum(part, axis)
    other = shift(part, "core", 1)
    return jnp.where(
        core == 0, jnp.concatenate([part, other]), jnp.concatenate([other, part])
    )


def on_device(
    control,
    perturbations,
    zonal_flow,
    meridional_flow,
    diffusivity,
    send_cell,
    send_station,
    send_weight,
    send_count,
    obs_value,
    obs_error,
):
    member_count = perturbations.shape[2]
    step_total, owned_count = obs_value.shape
    slots = send_cell.shape[3]
    size_z, size_x, size_c = (lax.axis_size(name) for name in COL)
    core = lax.axis_index("core")
    place = jnp.stack([lax.axis_index("z"), lax.axis_index("x")]).astype(jnp.int32)

    live = lax.broadcasted_iota(jnp.int32, send_cell.shape[2:], 1) < send_count[0, 0][:, None]
    station_live = jnp.where(live, send_station[0, 0], -1)
    whole_tables = jnp.concatenate(
        [
            send_cell[0, 0],
            station_live,
            jnp.broadcast_to(send_count[0, 0][:, None], (send_cell.shape[2], slots)),
        ],
        axis=1,
    ).reshape(size_z * size_x, size_c, 3 * slots)
    whole_weights = send_weight[0, 0].reshape(size_z * size_x, size_c, slots)
    index_own = lax.dynamic_index_in_dim(whole_tables, core, 1, keepdims=False)
    index_pair = shift(
        lax.dynamic_index_in_dim(whole_tables, 1 - core, 1, keepdims=False), "core", 1
    )
    weight_own = lax.dynamic_index_in_dim(whole_weights, core, 1, keepdims=False)
    weight_pair = shift(
        lax.dynamic_index_in_dim(whole_weights, 1 - core, 1, keepdims=False), "core", 1
    )

    zero = jnp.zeros_like(control)
    rates = jnp.stack(
        [
            diffusivity + jnp.maximum(-zonal_flow, 0.0),
            diffusivity + jnp.maximum(zonal_flow, 0.0),
            diffusivity + jnp.maximum(-meridional_flow, 0.0),
            diffusivity + jnp.maximum(meridional_flow, 0.0),
            control,
            zero,
            zero,
            zero,
        ],
        axis=1,
    ).reshape(-1, member_count, control.shape[1])
    first = advance(True, rates, perturbations, edges(perturbations + control[:, :, None]))
    second = advance(False, rates, first, edges(first))
    flat = [state.reshape(-1, member_count) for state in (first, second)]
    paired = [shift(state, "core", 1) for state in flat]
    index = jnp.concatenate([index_own, index_pair], axis=0)
    weight = jnp.concatenate([weight_own, weight_pair], axis=0)
    blocks = bin_rows(
        place,
        index[:, :slots].reshape(-1),
        weight.reshape(-1),
        index[:, 2 * slots],
        index[:, slots : 2 * slots],
        flat + paired,
        owned_count,
    )
    observed = reduce_to_owner(*blocks).reshape(step_total, owned_count, member_count)

    root_scale = math.sqrt(member_count - 1.0)
    obs_mean = jnp.mean(observed, axis=2)
    spread = observed - obs_mean[:, :, None]
    scaled = (spread / (obs_error[:, :, None] * root_scale)).reshape(-1, member_count)
    innovation = ((obs_value - obs_mean) / obs_error).reshape(-1)
    products = jnp.dot(
        jnp.concatenate(
            [scaled, innovation[:, None], jnp.zeros((scaled.shape[0], 15), jnp.float32)], axis=1
        ).T,
        scaled,
        precision=exact_mode,
    )
    products = sum_everywhere(products)
    high, low = transposed_weights(products, root_scale)
    analysis = analyse(high, low, flat[-1])
    obs_analysis = analyse(high, low, observed.reshape(-1, member_count))
    return (analysis.reshape(perturbations.shape), obs_analysis.reshape(observed.shape))


def solution(mesh):
    sizes = (mesh.shape["lat"], mesh.shape["col"] // 8, 4, 2)
    fine = Mesh(mesh.devices.reshape(sizes), ("lat",) + COL)
    grid = P("lat", COL)
    return jax.shard_map(
        on_device,
        mesh=fine,
        in_specs=(
            grid,
            P("lat", COL, None),
            grid,
            grid,
            grid,
            P("lat", COL, None, None),
            P("lat", COL, None, None),
            P("lat", COL, None, None),
            P("lat", COL, None),
            P(None, ("lat",) + COL),
            P(None, ("lat",) + COL),
        ),
        out_specs=(P("lat", COL, None), P(None, ("lat",) + COL, None)),
        check_vma=False,
    )
```

```python
import functools
import math

import jax
import jax.numpy as jnp
from jax import lax
from jax.experimental import pallas as pl
from jax.experimental.pallas import tpu as pltpu
from jax.sharding import Mesh
from jax.sharding import PartitionSpec as P

exact_mode = lax.Precision.HIGHEST
COL = ("z", "x", "core")
UNROLL = 16


def shift(value, axis, step):
    count = lax.axis_size(axis)
    return lax.ppermute(value, axis, [(i, (i + step) % count) for i in range(count)])


def neighbours(first_row, last_row, first_cell, last_cell):
    sides = []
    for axis, ends in (("lat", (last_row, first_row)), (COL, (last_cell, first_cell))):
        names = axis if isinstance(axis, tuple) else (axis,)
        count = math.prod(lax.axis_size(name) for name in names)
        forward = [(i, i + 1) for i in range(count - 1)]
        backward = [(target, source) for source, target in forward]
        sides.append(lax.ppermute(ends[0], axis, forward))
        sides.append(lax.ppermute(ends[1], axis, backward))
    return sides


def ends_of(block, offset=None):
    parts = []
    for dim in (0, 1):
        for start in (0, block.shape[dim] - 1):
            part = lax.slice_in_dim(block, start, start + 1, axis=dim)
            if offset is not None:
                part = part + lax.slice_in_dim(offset, start, start + 1, axis=dim)[:, :, None]
            parts.append(part)
    return parts


def advance_kernel(adds, rates, block, out, padded, turned):
    rows, cells, members = block.shape
    groups, lanes = rates.shape[0], rates.shape[1]
    per_group = rows // groups
    for group in range(groups):
        turned[group] = jnp.transpose(rates[group])
    nothing = jnp.zeros((cells, members), jnp.float32)
    padded[0, 8 : 8 + cells, :] = nothing
    padded[rows + 1, 8 : 8 + cells, :] = nothing

    def rate(i, kind):
        lane = (i % per_group) * (lanes // per_group) + kind
        index = jnp.full((cells, members), lane, jnp.int32)
        return jnp.take_along_axis(turned[i // per_group], index, axis=1)

    def fill(i, carry):
        value = block[i]
        padded[i + 1, 8 : 8 + cells, :] = value + rate(i, 4) if adds else value
        padded[i + 1, 0:8, :] = nothing[:8]
        padded[i + 1, 8 + cells : 16 + cells, :] = nothing[:8]
        return carry

    lax.fori_loop(0, rows, fill, 0)

    def row(i, carry):
        centre = padded[i + 1, 8 : 8 + cells, :]
        result = centre + rate(i, 0) * (padded[i + 2, 8 : 8 + cells, :] - centre)
        result = result + rate(i, 1) * (padded[i, 8 : 8 + cells, :] - centre)
        result = result + rate(i, 2) * (padded[i + 1, 9 : 9 + cells, :] - centre)
        out[i] = result + rate(i, 3) * (padded[i + 1, 7 : 7 + cells, :] - centre)
        return carry

    lax.fori_loop(0, rows, row, 0)


def advance(adds, rates, block):
    rows, cells, members = block.shape
    whole = pl.BlockSpec(memory_space=pltpu.VMEM)
    return pl.pallas_call(
        functools.partial(advance_kernel, adds),
        in_specs=[whole] * 2,
        out_specs=whole,
        out_shape=pltpu.VMEM(block.shape, jnp.float32),
        scratch_shapes=[
            pltpu.VMEM((rows + 2, cells + 16, members), jnp.float32),
            pltpu.VMEM((rates.shape[0], cells, rates.shape[1]), jnp.float32),
        ],
        compiler_params=pltpu.CompilerParams(vmem_limit_bytes=16 * 2**20),
        cost_estimate=pl.CostEstimate(
            flops=12 * block.size, bytes_accessed=8 * block.size, transcendentals=0
        ),
    )(rates, block)


def border_kernel(rates, above, below, left, right, block, out, lines):
    rows, cells, members = block.shape
    lanes = rates.shape[1]
    per_row = rates.shape[0] * lanes // rows
    first = jnp.transpose(rates[0, :per_row, :])
    last = jnp.transpose(rates[rates.shape[0] - 1, lanes - per_row :, :])
    out[0] = out[0] + first[:, 1:2] * above[0]
    out[rows - 1] = out[rows - 1] + last[:, 0:1] * below[0]
    flat = rates[...].reshape(rows * per_row, cells)
    lines[0] = jnp.broadcast_to(flat[:, 0:1], (rows * per_row, members))
    lines[1] = jnp.broadcast_to(flat[:, cells - 1 : cells], (rows * per_row, members))
    for i in range(rows):
        west, east = i * per_row + 3, i * per_row + 2
        out[i, 0:1, :] = out[i, 0:1, :] + lines[0, west : west + 1, :] * left[i]
        out[i, cells - 1 : cells, :] = (
            out[i, cells - 1 : cells, :] + lines[1, east : east + 1, :] * right[i]
        )


def with_border(rates, block, sides):
    whole = pl.BlockSpec(memory_space=pltpu.VMEM)
    lines = rates.shape[0] * rates.shape[1]
    return pl.pallas_call(
        border_kernel,
        in_specs=[whole] * 6,
        out_specs=whole,
        out_shape=pltpu.VMEM(block.shape, jnp.float32),
        input_output_aliases={5: 0},
        scratch_shapes=[pltpu.VMEM((2, lines, block.shape[2]), jnp.float32)],
        compiler_params=pltpu.CompilerParams(vmem_limit_bytes=4 * 2**20),
        cost_estimate=pl.CostEstimate(flops=10**6, bytes_accessed=2**20, transcendentals=0),
    )(rates, *sides, block)


def bin_kernel(x_major, size_z, size_x, owned, place, cell, weight, count, station, *rest):
    states, (out, picked) = rest[:2], rest[2:]
    width = out.shape[3]
    receivers, slots = size_z * size_x, station.shape[1]
    picked[...] = jnp.zeros_like(picked)
    own = lax.broadcasted_iota(jnp.int32, (owned, slots), 0)

    def one(step, carry):
        ahead_z, ahead_x = step // size_x, step % size_x
        receiver = ((place[0] + ahead_z) % size_z) * size_x + (place[1] + ahead_x) % size_x
        hots = []
        for e in range(2):
            entry = e * receivers + receiver

            def pick(group, inner):
                for j in range(UNROLL):
                    slot = entry * slots + group * UNROLL + j
                    tile, line = group * (UNROLL // 8) + j // 8, j % 8
                    picked[e, tile, line : line + 1, :] = (
                        states[e][pl.ds(cell[slot], 1), :] * weight[slot]
                    )
                return inner

            lax.fori_loop(0, (count[entry] + UNROLL - 1) // UNROLL, pick, 0)
            hit = station[pl.ds(entry, 1), :] == own
            hots.append(jnp.where(hit, 1.0, 0.0).astype(jnp.bfloat16))
        value = picked[...].reshape(2 * slots, width)
        high = value.astype(jnp.bfloat16)
        low = (value - high.astype(jnp.float32)).astype(jnp.bfloat16)
        total = jnp.dot(
            jnp.concatenate(hots, axis=1),
            jnp.concatenate([high, low], axis=1),
            preferred_element_type=jnp.float32,
        )
        total = total[:, :width] + total[:, width:]
        if x_major:
            out[ahead_x, ahead_z] = total
        else:
            out[ahead_z, ahead_x] = total
        return carry

    lax.fori_loop(0, receivers, one, 0)


def bin_rows(x_major, tables, states, owned):
    place, cell, weight, count, station = tables
    size_z, size_x = lax.axis_size("z"), lax.axis_size("x")
    members, slots = states[0].shape[1], station.shape[1]
    scalar = pl.BlockSpec(memory_space=pltpu.SMEM)
    whole = pl.BlockSpec(memory_space=pltpu.VMEM)
    sizes = (size_x, size_z) if x_major else (size_z, size_x)
    return pl.pallas_call(
        functools.partial(bin_kernel, x_major, size_z, size_x, owned),
        in_specs=[scalar] * 4 + [whole] * 3,
        out_specs=whole,
        out_shape=pltpu.VMEM(sizes + (owned, members), jnp.float32),
        scratch_shapes=[pltpu.VMEM((2, slots // 8, 8, members), jnp.float32)],
        compiler_params=pltpu.CompilerParams(vmem_limit_bytes=8 * 2**20),
        cost_estimate=pl.CostEstimate(
            flops=10**9, bytes_accessed=30 * 2**20, transcendentals=0
        ),
    )(place, cell, weight, count, station, *states)


def factor_kernel(root_scale, products, high, low):
    size = products.shape[1]
    lane = lax.broadcasted_iota(jnp.int32, (size, size), 1)
    line = lax.broadcasted_iota(jnp.int32, (size, size), 0)
    eye = jnp.where(lane == line, 1.0, 0.0)
    left, right = products[:size, :] + eye, eye
    width = 4
    done_left, done_right = [], []
    for start in range(0, size, width):
        top = start % 8
        columns = [
            jnp.broadcast_to(left[:, start + a : start + a + 1], left.shape) for a in range(width)
        ]
        pivots = [[columns[b][top + a : top + a + 1, :] for b in range(width)] for a in range(width)]
        upper = [[None] * width for _ in range(width)]
        inverse = []
        for a in range(width):
            lower = []
            for k in range(a):
                value = pivots[a][k]
                for m in range(k):
                    value = value - lower[m] * upper[m][k]
                lower.append(value * inverse[k])
            for b in range(a, width):
                value = pivots[a][b]
                for m in range(a):
                    value = value - lower[m] * upper[m][b]
                upper[a][b] = value
            inverse.append(1.0 / upper[a][a])
        below = line[: left.shape[0]]
        multipliers = []
        for a in range(width):
            value = columns[a]
            for m in range(a):
                value = value - multipliers[m] * upper[m][a]
            value = value * inverse[a]
            multipliers.append(jnp.where(below > top + a, value, 0.0))
        rows_left, rows_right = [], []
        for a in range(width):
            row_left = left[top + a : top + a + 1, :]
            row_right = right[top + a : top + a + 1, :]
            for m in range(a):
                scale = multipliers[m][top + a : top + a + 1, :]
                row_left = row_left - scale * rows_left[m]
                row_right = row_right - scale * rows_right[m]
            rows_left.append(row_left)
            rows_right.append(row_right)
        for m in range(width):
            left = left - multipliers[m] * rows_left[m]
            right = right - multipliers[m] * rows_right[m]
        if top + width == 8:
            done_left.append(left[:8])
            done_right.append(right[:8])
            left, right = left[8:], right[8:]
    left = jnp.concatenate(done_left, axis=0)
    right = jnp.concatenate(done_right, axis=0)
    pivot = jnp.sum(jnp.where(lane == line, left, 0.0), axis=1, keepdims=True)
    inverse = right * lax.rsqrt(pivot)
    push = products[size : size + 1, :]
    pushed = jnp.sum(inverse * push, axis=1, keepdims=True)
    offset = jnp.sum(inverse * pushed, axis=0, keepdims=True) * (1.0 / root_scale)
    weights = inverse + offset
    weights = weights - jnp.mean(weights, axis=1, keepdims=True) + 1.0 / size
    top_half = weights.astype(jnp.bfloat16)
    high[...] = top_half
    low[...] = (weights - top_half.astype(jnp.float32)).astype(jnp.bfloat16)


def transposed_weights(products, root_scale):
    size = products.shape[1]
    whole = pl.BlockSpec(memory_space=pltpu.VMEM)
    return pl.pallas_call(
        functools.partial(factor_kernel, root_scale),
        in_specs=[whole],
        out_specs=[whole] * 2,
        out_shape=[jax.ShapeDtypeStruct((size, size), jnp.bfloat16)] * 2,
    )(products)


def analysis_kernel(size, high, low, state, observed, out, out_observed):
    def update(value):
        near = value.astype(jnp.bfloat16)
        rest = (value - near.astype(jnp.float32)).astype(jnp.bfloat16)

        def times(a, b):
            return lax.dot_general(
                a, b[...], (((1,), (1,)), ((), ())), preferred_element_type=jnp.float32
            )

        return times(near, high) + (times(rest, high) + times(near, low))

    step = pl.program_id(0)
    out[...] = update(state[pl.ds(pl.multiple_of(step * size, size), size), :])

    @pl.when(step == 0)
    def _():
        out_observed[...] = update(observed[...])


def analyse(high, low, state, observed):
    rows, members = state.shape
    size = rows // 8
    whole = pl.BlockSpec(memory_space=pltpu.VMEM)
    return pl.pallas_call(
        functools.partial(analysis_kernel, size),
        grid=(rows // size,),
        in_specs=[whole] * 4,
        out_specs=[
            pl.BlockSpec((size, members), lambda k: (k, 0)),
            pl.BlockSpec(observed.shape, lambda k: (0, 0)),
        ],
        out_shape=[
            jax.ShapeDtypeStruct(state.shape, jnp.float32),
            jax.ShapeDtypeStruct(observed.shape, jnp.float32),
        ],
        compiler_params=pltpu.CompilerParams(vmem_limit_bytes=16 * 2**20),
    )(high, low, state, observed)


def ring_reduce(blocks, axis):
    count = len(blocks)
    half = count // 2
    cut = blocks[half].shape[-2] // 2
    up = shift(blocks[half][..., :cut, :], axis, 1)
    down = shift(blocks[half][..., cut:, :], axis, -1)
    ahead, behind = blocks[half - 1], blocks[count - half + 1]
    up = jnp.concatenate([ahead[..., :cut, :] + up, ahead[..., cut:, :]], axis=-2)
    down = jnp.concatenate([behind[..., :cut, :], behind[..., cut:, :] + down], axis=-2)
    for k in range(half - 1, 0, -1):
        up = shift(up, axis, 1)
        down = shift(down, axis, -1)
        if k > 1:
            up = blocks[k - 1] + up
            down = blocks[count - k + 1] + down
    return blocks[0] + up + down


def reduce_x_then_z(blocks):
    part = ring_reduce([blocks[k] for k in range(blocks.shape[0])], "x")
    return ring_reduce([part[k] for k in range(part.shape[0])], "z")


def reduce_z_then_x(blocks):
    part = ring_reduce([blocks[k] for k in range(blocks.shape[0])], "z")
    return ring_reduce([part[k] for k in range(part.shape[0])], "x")


def member_products(observed, value, error, root_scale):
    mean = jnp.mean(observed, axis=1)
    scaled = (observed - mean[:, None]) / (error[:, None] * root_scale)
    innovation = (value - mean) / error
    padding = jnp.zeros((scaled.shape[0], 15), jnp.float32)
    left = jnp.concatenate([scaled, innovation[:, None], padding], axis=1)
    return jnp.dot(left.T, scaled, precision=exact_mode)


def spread_sum(value, axis):
    count = lax.axis_size(axis)
    copies = jnp.broadcast_to(value[None], (count,) + value.shape)
    return jnp.sum(lax.all_to_all(copies, axis, split_axis=0, concat_axis=0, tiled=True), axis=0)


def sum_everywhere(value):
    core = lax.axis_index("core")
    rows = value.shape[0] // 2
    value = value + shift(value, "core", 1)
    part = lax.dynamic_slice_in_dim(value, core * rows, rows, 0)
    for axis in ("x", "lat", "z"):
        part = spread_sum(part, axis)
    other = shift(part, "core", 1)
    return jnp.where(
        core == 0, jnp.concatenate([part, other]), jnp.concatenate([other, part])
    )


def on_device(
    control,
    perturbations,
    zonal_flow,
    meridional_flow,
    diffusivity,
    send_cell,
    send_station,
    send_weight,
    send_count,
    obs_value,
    obs_error,
):
    member_count = perturbations.shape[2]
    step_total, owned_count = obs_value.shape
    slots = send_cell.shape[3]
    size_z, size_x, size_c = (lax.axis_size(name) for name in COL)
    core = lax.axis_index("core")
    place = jnp.stack([lax.axis_index("z"), lax.axis_index("x")]).astype(jnp.int32)

    live = lax.broadcasted_iota(jnp.int32, send_cell.shape[2:], 1) < send_count[0, 0][:, None]
    station_live = jnp.where(live, send_station[0, 0], -1)
    whole_tables = jnp.concatenate(
        [
            send_cell[0, 0],
            station_live,
            jnp.broadcast_to(send_count[0, 0][:, None], (send_cell.shape[2], slots)),
        ],
        axis=1,
    ).reshape(size_z * size_x, size_c, 3 * slots)
    whole_weights = send_weight[0, 0].reshape(size_z * size_x, size_c, slots)
    index_own = lax.dynamic_index_in_dim(whole_tables, core, 1, keepdims=False)
    index_pair = shift(
        lax.dynamic_index_in_dim(whole_tables, 1 - core, 1, keepdims=False), "core", 1
    )
    weight_own = lax.dynamic_index_in_dim(whole_weights, core, 1, keepdims=False)
    weight_pair = shift(
        lax.dynamic_index_in_dim(whole_weights, 1 - core, 1, keepdims=False), "core", 1
    )

    zero = jnp.zeros_like(control)
    rates = jnp.stack(
        [
            diffusivity + jnp.maximum(-zonal_flow, 0.0),
            diffusivity + jnp.maximum(zonal_flow, 0.0),
            diffusivity + jnp.maximum(-meridional_flow, 0.0),
            diffusivity + jnp.maximum(meridional_flow, 0.0),
            control,
            zero,
            zero,
            zero,
        ],
        axis=1,
    ).reshape(-1, member_count, control.shape[1])
    index = jnp.concatenate([index_own, index_pair], axis=0)
    weight = jnp.concatenate([weight_own, weight_pair], axis=0)
    tables = (
        place,
        index[:, :slots].reshape(-1),
        weight.reshape(-1),
        index[:, 2 * slots],
        index[:, slots : 2 * slots],
    )
    sides = neighbours(*ends_of(perturbations, control))
    first = advance(True, rates, perturbations)
    first, tables, sides = lax.optimization_barrier((first, tables, sides))
    first = with_border(rates, first, sides)
    flat_first = first.reshape(-1, member_count)
    pair_first = shift(flat_first, "core", 1)
    sides = neighbours(*ends_of(first))
    second = with_border(rates, advance(False, rates, first), sides)
    flat_second = second.reshape(-1, member_count)
    pair_second = shift(flat_second, "core", 1)

    root_scale = math.sqrt(member_count - 1.0)
    blocks_first = bin_rows(True, tables, (flat_first, pair_first), owned_count)
    blocks_second = bin_rows(False, tables, (flat_second, pair_second), owned_count)
    observed_first = reduce_x_then_z(blocks_first)
    observed_second = reduce_z_then_x(blocks_second)
    products = member_products(observed_first, obs_value[0], obs_error[0], root_scale)
    products = products + member_products(
        observed_second, obs_value[1], obs_error[1], root_scale
    )
    high, low = transposed_weights(sum_everywhere(products), root_scale)
    observed = jnp.concatenate([observed_first, observed_second], axis=0)
    analysis, obs_analysis = analyse(high, low, flat_second, observed)
    return (
        analysis.reshape(perturbations.shape),
        obs_analysis.reshape(step_total, owned_count, member_count),
    )


def solution(mesh):
    sizes = (mesh.shape["lat"], mesh.shape["col"] // 8, 4, 2)
    fine = Mesh(mesh.devices.reshape(sizes), ("lat",) + COL)
    grid = P("lat", COL)
    return jax.shard_map(
        on_device,
        mesh=fine,
        in_specs=(
            grid,
            P("lat", COL, None),
            grid,
            grid,
            grid,
            P("lat", COL, None, None),
            P("lat", COL, None, None),
            P("lat", COL, None, None),
            P("lat", COL, None),
            P(None, ("lat",) + COL),
            P(None, ("lat",) + COL),
        ),
        out_specs=(P("lat", COL, None), P(None, ("lat",) + COL, None)),
        check_vma=False,
    )
```

```python
import functools
import math

import jax
import jax.numpy as jnp
import numpy as np
from jax import lax
from jax.experimental import pallas as pl
from jax.experimental.pallas import tpu as pltpu
from jax.sharding import Mesh
from jax.sharding import PartitionSpec as P

exact_mode = lax.Precision.HIGHEST
COL = ("z", "x", "core")
UNROLL = 16


def shift(value, axis, step):
    count = lax.axis_size(axis)
    return lax.ppermute(value, axis, [(i, (i + step) % count) for i in range(count)])


def swap(value):
    return shift(value, "core", 1)


def onward(value, axis):
    count = lax.axis_size(axis)
    pairs = []
    for i in range(count):
        pairs += [(2 * i, 2 * ((i + 1) % count)), (2 * i + 1, 2 * ((i - 1) % count) + 1)]
    return lax.ppermute(value, (axis, "core"), pairs)


def neighbours(first_row, last_row, first_cell, last_cell):
    sides = []
    for axis, ends in (("lat", (last_row, first_row)), (COL, (last_cell, first_cell))):
        names = axis if isinstance(axis, tuple) else (axis,)
        count = math.prod(lax.axis_size(name) for name in names)
        forward = [(i, i + 1) for i in range(count - 1)]
        backward = [(target, source) for source, target in forward]
        sides.append(lax.ppermute(ends[0], axis, forward))
        sides.append(lax.ppermute(ends[1], axis, backward))
    return sides


def ends_of(block, offset=None):
    parts = []
    for dim in (0, 1):
        for start in (0, block.shape[dim] - 1):
            part = lax.slice_in_dim(block, start, start + 1, axis=dim)
            if offset is not None:
                part = part + lax.slice_in_dim(offset, start, start + 1, axis=dim)[:, :, None]
            parts.append(part)
    return parts


def upwind_rates(zonal, meridional, diffusion):
    return [
        diffusion + jnp.maximum(-zonal, 0.0),
        diffusion + jnp.maximum(zonal, 0.0),
        diffusion + jnp.maximum(-meridional, 0.0),
        diffusion + jnp.maximum(meridional, 0.0),
    ]


def advance_kernel(adds, control, zonal, meridional, diffusion, block, out, padded, turned):
    rows, cells, members = block.shape
    rates = upwind_rates(zonal[...], meridional[...], diffusion[...])
    turned[0] = jnp.transpose(jnp.concatenate(rates, axis=0))
    if adds:
        turned[1] = jnp.transpose(jnp.concatenate([control[...]] * 4, axis=0))
    nothing = jnp.zeros((cells, members), jnp.float32)
    padded[0, 8 : 8 + cells, :] = nothing
    padded[rows + 1, 8 : 8 + cells, :] = nothing

    def rate(i, kind):
        lane = (kind % 4) * rows + i
        index = jnp.full((cells, members), lane, jnp.int32)
        return jnp.take_along_axis(turned[kind // 4], index, axis=1)

    def fill(i, carry):
        value = block[i]
        padded[i + 1, 8 : 8 + cells, :] = value + rate(i, 4) if adds else value
        padded[i + 1, 0:8, :] = nothing[:8]
        padded[i + 1, 8 + cells : 16 + cells, :] = nothing[:8]
        return carry

    lax.fori_loop(0, rows, fill, 0)

    def row(i, carry):
        centre = padded[i + 1, 8 : 8 + cells, :]
        result = centre + rate(i, 0) * (padded[i + 2, 8 : 8 + cells, :] - centre)
        result = result + rate(i, 1) * (padded[i, 8 : 8 + cells, :] - centre)
        result = result + rate(i, 2) * (padded[i + 1, 9 : 9 + cells, :] - centre)
        out[i] = result + rate(i, 3) * (padded[i + 1, 7 : 7 + cells, :] - centre)
        return carry

    lax.fori_loop(0, rows, row, 0)


def advance(adds, fields, block):
    rows, cells, members = block.shape
    whole = pl.BlockSpec(memory_space=pltpu.VMEM)
    return pl.pallas_call(
        functools.partial(advance_kernel, adds),
        in_specs=[whole] * 5,
        out_specs=whole,
        out_shape=pltpu.VMEM(block.shape, jnp.float32),
        scratch_shapes=[
            pltpu.VMEM((rows + 2, cells + 16, members), jnp.float32),
            pltpu.VMEM((2, cells, 4 * rows), jnp.float32),
        ],
        compiler_params=pltpu.CompilerParams(vmem_limit_bytes=16 * 2**20),
        cost_estimate=pl.CostEstimate(
            flops=12 * block.size, bytes_accessed=8 * block.size, transcendentals=0
        ),
    )(*fields, block)


def border_kernel(zonal, meridional, diffusion, above, below, left, right, block, out, lines):
    rows, cells, members = block.shape

    def copy(i, carry):
        out[i] = block[i]
        return carry

    lax.fori_loop(0, rows, copy, 0)
    east, west, north, south = upwind_rates(zonal[...], meridional[...], diffusion[...])
    first = jnp.transpose(west[0:8, :])
    last = jnp.transpose(east[rows - 8 : rows, :])
    out[0] = out[0] + first[:, 0:1] * above[0]
    out[rows - 1] = out[rows - 1] + last[:, 7:8] * below[0]
    lines[0] = jnp.broadcast_to(south[:, 0:1], (rows, members))
    lines[1] = jnp.broadcast_to(north[:, cells - 1 : cells], (rows, members))
    for i in range(rows):
        out[i, 0:1, :] = out[i, 0:1, :] + lines[0, i : i + 1, :] * left[i]
        out[i, cells - 1 : cells, :] = (
            out[i, cells - 1 : cells, :] + lines[1, i : i + 1, :] * right[i]
        )


def with_border(fields, block, sides):
    whole = pl.BlockSpec(memory_space=pltpu.VMEM)
    return pl.pallas_call(
        border_kernel,
        in_specs=[whole] * 8,
        out_specs=whole,
        out_shape=pltpu.VMEM(block.shape, jnp.float32),
        scratch_shapes=[pltpu.VMEM((2, block.shape[0], block.shape[2]), jnp.float32)],
        compiler_params=pltpu.CompilerParams(vmem_limit_bytes=12 * 2**20),
        cost_estimate=pl.CostEstimate(flops=10**6, bytes_accessed=2**20, transcendentals=0),
    )(*fields[1:], *sides, block)


def bin_kernel(owned, receivers, cells, weights, counts, *refs):
    stations, states, (out, picked) = refs[:2], refs[2:4], refs[4:]
    width, slots = out.shape[2], stations[0].shape[1]
    picked[...] = jnp.zeros_like(picked)
    own = lax.broadcasted_iota(jnp.int32, (owned, slots), 0)
    order = lax.broadcasted_iota(jnp.int32, (1, slots), 1)

    def one(step, carry):
        receiver = receivers[step]
        hots = []
        for e in range(2):
            entry = e * stations[e].shape[0] + receiver
            live = counts[entry]

            def pick(group, inner):
                for j in range(UNROLL):
                    slot = entry * slots + group * UNROLL + j
                    tile, line = group * (UNROLL // 8) + j // 8, j % 8
                    picked[e, tile, line : line + 1, :] = (
                        states[e][pl.ds(cells[slot], 1), :] * weights[slot]
                    )
                return inner

            lax.fori_loop(0, (live + UNROLL - 1) // UNROLL, pick, 0)
            station = jnp.where(order < live, stations[e][pl.ds(receiver, 1), :], -1)
            hots.append(jnp.where(station == own, 1.0, 0.0).astype(jnp.bfloat16))
        value = picked[...].reshape(2 * slots, width)
        high = value.astype(jnp.bfloat16)
        low = (value - high.astype(jnp.float32)).astype(jnp.bfloat16)
        total = jnp.dot(
            jnp.concatenate(hots, axis=1),
            jnp.concatenate([high, low], axis=1),
            preferred_element_type=jnp.float32,
        )
        out[step] = total[:, :width] + total[:, width:]
        return carry

    lax.fori_loop(0, out.shape[0], one, 0)


def bin_rows(receivers, tables, states, owned):
    members, slots = states[0].shape[1], tables[-1].shape[1]
    scalar = pl.BlockSpec(memory_space=pltpu.SMEM)
    whole = pl.BlockSpec(memory_space=pltpu.VMEM)
    return pl.pallas_call(
        functools.partial(bin_kernel, owned),
        in_specs=[scalar] * 4 + [whole] * 4,
        out_specs=whole,
        out_shape=pltpu.VMEM((receivers.shape[0], owned, members), jnp.float32),
        scratch_shapes=[pltpu.VMEM((2, slots // 8, 8, members), jnp.float32)],
        compiler_params=pltpu.CompilerParams(vmem_limit_bytes=14 * 2**20),
        cost_estimate=pl.CostEstimate(
            flops=10**9, bytes_accessed=30 * 2**20, transcendentals=0
        ),
    )(receivers, *tables, *states)


def factor_kernel(root_scale, products, high, low):
    size = products.shape[1]
    lane = lax.broadcasted_iota(jnp.int32, (size, size), 1)
    line = lax.broadcasted_iota(jnp.int32, (size, size), 0)
    eye = jnp.where(lane == line, 1.0, 0.0)
    left, right = products[:size, :] + eye, eye
    width = 4
    done_left, done_right = [], []
    for start in range(0, size, width):
        top = start % 8
        columns = [
            jnp.broadcast_to(left[:, start + a : start + a + 1], left.shape) for a in range(width)
        ]
        pivots = [[columns[b][top + a : top + a + 1, :] for b in range(width)] for a in range(width)]
        upper = [[None] * width for _ in range(width)]
        inverse = []
        for a in range(width):
            lower = []
            for k in range(a):
                value = pivots[a][k]
                for m in range(k):
                    value = value - lower[m] * upper[m][k]
                lower.append(value * inverse[k])
            for b in range(a, width):
                value = pivots[a][b]
                for m in range(a):
                    value = value - lower[m] * upper[m][b]
                upper[a][b] = value
            inverse.append(1.0 / upper[a][a])
        below = line[: left.shape[0]]
        multipliers = []
        for a in range(width):
            value = columns[a]
            for m in range(a):
                value = value - multipliers[m] * upper[m][a]
            value = value * inverse[a]
            multipliers.append(jnp.where(below > top + a, value, 0.0))
        rows_left, rows_right = [], []
        for a in range(width):
            row_left = left[top + a : top + a + 1, :]
            row_right = right[top + a : top + a + 1, :]
            for m in range(a):
                scale = multipliers[m][top + a : top + a + 1, :]
                row_left = row_left - scale * rows_left[m]
                row_right = row_right - scale * rows_right[m]
            rows_left.append(row_left)
            rows_right.append(row_right)
        for m in range(width):
            left = left - multipliers[m] * rows_left[m]
            right = right - multipliers[m] * rows_right[m]
        if top + width == 8:
            done_left.append(left[:8])
            done_right.append(right[:8])
            left, right = left[8:], right[8:]
    left = jnp.concatenate(done_left, axis=0)
    right = jnp.concatenate(done_right, axis=0)
    pivot = jnp.sum(jnp.where(lane == line, left, 0.0), axis=1, keepdims=True)
    inverse = right * lax.rsqrt(pivot)
    push = products[size : size + 1, :]
    pushed = jnp.sum(inverse * push, axis=1, keepdims=True)
    offset = jnp.sum(inverse * pushed, axis=0, keepdims=True) * (1.0 / root_scale)
    weights = inverse + offset
    weights = weights - jnp.mean(weights, axis=1, keepdims=True) + 1.0 / size
    top_half = weights.astype(jnp.bfloat16)
    high[...] = top_half
    low[...] = (weights - top_half.astype(jnp.float32)).astype(jnp.bfloat16)


def transposed_weights(products, root_scale):
    size = products.shape[1]
    whole = pl.BlockSpec(memory_space=pltpu.VMEM)
    return pl.pallas_call(
        functools.partial(factor_kernel, root_scale),
        in_specs=[whole],
        out_specs=[whole] * 2,
        out_shape=[pltpu.VMEM((size, size), jnp.bfloat16)] * 2,
    )(products)


def analysis_kernel(high, low, state, observed, out, out_observed):
    def update(value):
        near = value.astype(jnp.bfloat16)
        rest = (value - near.astype(jnp.float32)).astype(jnp.bfloat16)

        def times(a, b):
            return lax.dot_general(
                a, b[...], (((1,), (1,)), ((), ())), preferred_element_type=jnp.float32
            )

        return times(near, high) + (times(rest, high) + times(near, low))

    size = out.shape[0]
    start = pl.multiple_of(pl.program_id(0) * size, size)
    out[...] = update(state[pl.ds(start, size), :])

    @pl.when(pl.program_id(0) == 0)
    def _():
        out_observed[...] = update(observed[...])


def analyse(high, low, state, observed):
    rows, members = state.shape
    size = rows // 8
    whole = pl.BlockSpec(memory_space=pltpu.VMEM)
    block = pl.BlockSpec((size, members), lambda k: (k, 0))
    return pl.pallas_call(
        analysis_kernel,
        grid=(rows // size,),
        in_specs=[whole] * 4,
        out_specs=[block, pl.BlockSpec(observed.shape, lambda k: (0, 0))],
        out_shape=[
            jax.ShapeDtypeStruct(state.shape, jnp.float32),
            jax.ShapeDtypeStruct(observed.shape, jnp.float32),
        ],
        compiler_params=pltpu.CompilerParams(vmem_limit_bytes=16 * 2**20),
    )(high, low, state, observed)


def stage_entries(count):
    entries = [(count // 2, 0)]
    for distance in range(count // 2 - 1, 0, -1):
        entries += [(distance, 0), (distance, 1)]
    return entries + [(0, 0)]


def stage(held, axis):
    count = lax.axis_size(axis)
    moving = onward(held[0], axis)
    for distance in range(count // 2 - 1, 0, -1):
        start = 2 * (count // 2 - 1 - distance) + 1
        pair = held[start : start + 2]
        if distance == count // 2 - 1:
            pair = jnp.stack([pair[0] + moving, pair[1]])
        else:
            pair = pair + moving
        moving = onward(pair, axis)
    return moving[0] + held[-1], moving[1]


def reduce_to_owner(blocks, first_axis, second_axis):
    count = lax.axis_size(second_axis)
    mine, others = stage(blocks.reshape((-1, count) + blocks.shape[1:]), first_axis)
    keep, give = [], []
    for distance, whose in stage_entries(count):
        keep.append((mine, others)[whose][distance])
        give.append((others, mine)[whose][-distance % count])
    held = jnp.stack(keep) + swap(jnp.stack(give))
    mine, others = stage(held, second_axis)
    return mine + swap(others)


def receiver_list(first_axis, second_axis):
    core = lax.axis_index("core")
    direction = 1 - 2 * core
    at = {name: lax.axis_index(name) for name in COL}
    size = {name: lax.axis_size(name) for name in COL}
    entries = stage_entries(size[first_axis])
    count = size[second_axis]
    ahead = np.repeat([entry[0] for entry in entries], count)
    whose = np.repeat([entry[1] for entry in entries], count)
    along = np.tile(np.arange(count), len(entries))
    place = {
        first_axis: (at[first_axis] + direction * ahead) % size[first_axis],
        second_axis: (at[second_axis] + direction * along) % size[second_axis],
    }
    chip = place["z"] * size["x"] + place["x"]
    return (chip * size["core"] + (core + whose) % 2).astype(jnp.int32)


def member_products(observed, value, error, root_scale):
    mean = jnp.mean(observed, axis=1)
    scaled = (observed - mean[:, None]) / (error[:, None] * root_scale)
    innovation = (value - mean) / error
    padding = jnp.zeros((scaled.shape[0], 15), jnp.float32)
    left = jnp.concatenate([scaled, innovation[:, None], padding], axis=1)
    return jnp.dot(left.T, scaled, precision=exact_mode)


def spread_sum(value, axis):
    count = lax.axis_size(axis)
    copies = jnp.broadcast_to(value[None], (count,) + value.shape)
    return jnp.sum(lax.all_to_all(copies, axis, split_axis=0, concat_axis=0, tiled=True), axis=0)


def sum_everywhere(value):
    core = lax.axis_index("core")
    rows = value.shape[0] // 2
    value = value + shift(value, "core", 1)
    part = lax.dynamic_slice_in_dim(value, core * rows, rows, 0)
    for axis in ("x", "lat", "z"):
        part = spread_sum(part, axis)
    other = shift(part, "core", 1)
    return jnp.where(
        core == 0, jnp.concatenate([part, other]), jnp.concatenate([other, part])
    )


def on_device(
    control,
    perturbations,
    zonal_flow,
    meridional_flow,
    diffusivity,
    send_cell,
    send_station,
    send_weight,
    send_count,
    obs_value,
    obs_error,
):
    member_count = perturbations.shape[2]
    step_total, owned_count = obs_value.shape
    fields = (control, zonal_flow, meridional_flow, diffusivity)

    sides = neighbours(*ends_of(perturbations, control))
    tables = [
        jnp.concatenate([table[0, 0], swap(table[0, 0])], axis=0).reshape(-1)
        for table in (send_cell, send_weight, send_count)
    ]
    tables += [send_station[0, 0], swap(send_station[0, 0])]
    first = advance(True, fields, perturbations)
    first, tables, sides = lax.optimization_barrier((first, tables, sides))
    first = with_border(fields, first, sides)
    flat_first = first.reshape(-1, member_count)
    pair_first = swap(flat_first)
    sides = neighbours(*ends_of(first))
    second = with_border(fields, advance(False, fields, first), sides)
    flat_second = second.reshape(-1, member_count)
    pair_second = swap(flat_second)

    root_scale = math.sqrt(member_count - 1.0)
    blocks = bin_rows(receiver_list("x", "z"), tables, (flat_first, pair_first), owned_count)
    observed_first = reduce_to_owner(blocks, "x", "z")
    blocks = bin_rows(receiver_list("z", "x"), tables, (flat_second, pair_second), owned_count)
    observed_second = reduce_to_owner(blocks, "z", "x")
    products = member_products(observed_first, obs_value[0], obs_error[0], root_scale)
    products = products + member_products(
        observed_second, obs_value[1], obs_error[1], root_scale
    )
    high, low = transposed_weights(sum_everywhere(products), root_scale)
    observed = jnp.concatenate([observed_first, observed_second], axis=0)
    analysis, obs_analysis = analyse(high, low, flat_second, observed)
    return (
        analysis.reshape(perturbations.shape),
        obs_analysis.reshape(step_total, owned_count, member_count),
    )


def solution(mesh):
    sizes = (mesh.shape["lat"], mesh.shape["col"] // 8, 4, 2)
    fine = Mesh(mesh.devices.reshape(sizes), ("lat",) + COL)
    grid = P("lat", COL)
    return jax.shard_map(
        on_device,
        mesh=fine,
        in_specs=(
            grid,
            P("lat", COL, None),
            grid,
            grid,
            grid,
            P("lat", COL, None, None),
            P("lat", COL, None, None),
            P("lat", COL, None, None),
            P("lat", COL, None),
            P(None, ("lat",) + COL),
            P(None, ("lat",) + COL),
        ),
        out_specs=(P("lat", COL, None), P(None, ("lat",) + COL, None)),
        check_vma=False,
    )
```

```python
import functools
import math

import jax
import jax.numpy as jnp
import numpy as np
from jax import lax
from jax.experimental import pallas as pl
from jax.experimental.pallas import tpu as pltpu
from jax.sharding import Mesh
from jax.sharding import PartitionSpec as P

exact_mode = lax.Precision.HIGHEST
COL = ("z", "x", "core")
UNROLL = 16


def shift(value, axis, step):
    count = lax.axis_size(axis)
    return lax.ppermute(value, axis, [(i, (i + step) % count) for i in range(count)])


def swap(value):
    return shift(value, "core", 1)


def onward(value, axis):
    count = lax.axis_size(axis)
    pairs = []
    for i in range(count):
        pairs += [(2 * i, 2 * ((i + 1) % count)), (2 * i + 1, 2 * ((i - 1) % count) + 1)]
    return lax.ppermute(value, (axis, "core"), pairs)


def neighbours(first_row, last_row, first_cell, last_cell):
    sides = []
    for axis, ends in (("lat", (last_row, first_row)), (COL, (last_cell, first_cell))):
        names = axis if isinstance(axis, tuple) else (axis,)
        count = math.prod(lax.axis_size(name) for name in names)
        forward = [(i, i + 1) for i in range(count - 1)]
        backward = [(target, source) for source, target in forward]
        sides.append(lax.ppermute(ends[0], axis, forward))
        sides.append(lax.ppermute(ends[1], axis, backward))
    return sides


def ends_of(block, offset=None):
    parts = []
    for dim in (0, 1):
        for start in (0, block.shape[dim] - 1):
            part = lax.slice_in_dim(block, start, start + 1, axis=dim)
            if offset is not None:
                part = part + lax.slice_in_dim(offset, start, start + 1, axis=dim)[:, :, None]
            parts.append(part)
    return parts


def upwind_rates(zonal, meridional, diffusion):
    return [
        diffusion + jnp.maximum(-zonal, 0.0),
        diffusion + jnp.maximum(zonal, 0.0),
        diffusion + jnp.maximum(-meridional, 0.0),
        diffusion + jnp.maximum(meridional, 0.0),
    ]


def advance_kernel(adds, control, zonal, meridional, diffusion, block, out, padded, turned):
    rows, cells, members = block.shape
    rates = upwind_rates(zonal[...], meridional[...], diffusion[...])
    turned[0] = jnp.transpose(jnp.concatenate(rates, axis=0))
    if adds:
        turned[1] = jnp.transpose(jnp.concatenate([control[...]] * 4, axis=0))
    nothing = jnp.zeros((cells, members), jnp.float32)
    padded[0, 8 : 8 + cells, :] = nothing
    padded[rows + 1, 8 : 8 + cells, :] = nothing

    def rate(i, kind):
        lane = (kind % 4) * rows + i
        index = jnp.full((cells, members), lane, jnp.int32)
        return jnp.take_along_axis(turned[kind // 4], index, axis=1)

    def fill(i, carry):
        value = block[i]
        padded[i + 1, 8 : 8 + cells, :] = value + rate(i, 4) if adds else value
        padded[i + 1, 0:8, :] = nothing[:8]
        padded[i + 1, 8 + cells : 16 + cells, :] = nothing[:8]
        return carry

    lax.fori_loop(0, rows, fill, 0)

    def row(i, carry):
        centre = padded[i + 1, 8 : 8 + cells, :]
        result = centre + rate(i, 0) * (padded[i + 2, 8 : 8 + cells, :] - centre)
        result = result + rate(i, 1) * (padded[i, 8 : 8 + cells, :] - centre)
        result = result + rate(i, 2) * (padded[i + 1, 9 : 9 + cells, :] - centre)
        out[i] = result + rate(i, 3) * (padded[i + 1, 7 : 7 + cells, :] - centre)
        return carry

    lax.fori_loop(0, rows, row, 0)


def advance(adds, fields, block):
    rows, cells, members = block.shape
    whole = pl.BlockSpec(memory_space=pltpu.VMEM)
    return pl.pallas_call(
        functools.partial(advance_kernel, adds),
        in_specs=[whole] * 5,
        out_specs=whole,
        out_shape=pltpu.VMEM(block.shape, jnp.float32),
        scratch_shapes=[
            pltpu.VMEM((rows + 2, cells + 16, members), jnp.float32),
            pltpu.VMEM((2, cells, 4 * rows), jnp.float32),
        ],
        compiler_params=pltpu.CompilerParams(vmem_limit_bytes=16 * 2**20),
        cost_estimate=pl.CostEstimate(
            flops=12 * block.size, bytes_accessed=8 * block.size, transcendentals=0
        ),
    )(*fields, block)


def border_kernel(zonal, meridional, diffusion, above, below, left, right, block, out, lines):
    rows, cells, members = block.shape

    def copy(i, carry):
        out[i] = block[i]
        return carry

    lax.fori_loop(0, rows, copy, 0)
    east, west, north, south = upwind_rates(zonal[...], meridional[...], diffusion[...])
    first = jnp.transpose(west[0:8, :])
    last = jnp.transpose(east[rows - 8 : rows, :])
    out[0] = out[0] + first[:, 0:1] * above[0]
    out[rows - 1] = out[rows - 1] + last[:, 7:8] * below[0]
    lines[0] = jnp.broadcast_to(south[:, 0:1], (rows, members))
    lines[1] = jnp.broadcast_to(north[:, cells - 1 : cells], (rows, members))
    for i in range(rows):
        out[i, 0:1, :] = out[i, 0:1, :] + lines[0, i : i + 1, :] * left[i]
        out[i, cells - 1 : cells, :] = (
            out[i, cells - 1 : cells, :] + lines[1, i : i + 1, :] * right[i]
        )


def with_border(fields, block, sides):
    whole = pl.BlockSpec(memory_space=pltpu.VMEM)
    return pl.pallas_call(
        border_kernel,
        in_specs=[whole] * 8,
        out_specs=whole,
        out_shape=pltpu.VMEM(block.shape, jnp.float32),
        scratch_shapes=[pltpu.VMEM((2, block.shape[0], block.shape[2]), jnp.float32)],
        compiler_params=pltpu.CompilerParams(vmem_limit_bytes=12 * 2**20),
        cost_estimate=pl.CostEstimate(flops=10**6, bytes_accessed=2**20, transcendentals=0),
    )(*fields[1:], *sides, block)


def bin_kernel(owned, receivers, cells, weights, counts, *refs):
    stations, states, (out, picked) = refs[:2], refs[2:4], refs[4:]
    width, slots = out.shape[2], stations[0].shape[1]
    picked[...] = jnp.zeros_like(picked)
    own = lax.broadcasted_iota(jnp.int32, (owned, slots), 0)
    order = lax.broadcasted_iota(jnp.int32, (1, slots), 1)

    def one(step, carry):
        receiver = receivers[step]
        hots = []
        for e in range(2):
            entry = e * stations[e].shape[0] + receiver
            live = counts[entry]

            def pick(group, inner):
                for j in range(UNROLL):
                    slot = entry * slots + group * UNROLL + j
                    tile, line = group * (UNROLL // 8) + j // 8, j % 8
                    picked[e, tile, line : line + 1, :] = (
                        states[e][pl.ds(cells[slot], 1), :] * weights[slot]
                    )
                return inner

            lax.fori_loop(0, (live + UNROLL - 1) // UNROLL, pick, 0)
            station = jnp.where(order < live, stations[e][pl.ds(receiver, 1), :], -1)
            hots.append(jnp.where(station == own, 1.0, 0.0).astype(jnp.bfloat16))
        value = picked[...].reshape(2 * slots, width)
        high = value.astype(jnp.bfloat16)
        low = (value - high.astype(jnp.float32)).astype(jnp.bfloat16)
        total = jnp.dot(
            jnp.concatenate(hots, axis=1),
            jnp.concatenate([high, low], axis=1),
            preferred_element_type=jnp.float32,
        )
        out[step] = total[:, :width] + total[:, width:]
        return carry

    lax.fori_loop(0, out.shape[0], one, 0)


def bin_rows(receivers, tables, states, owned):
    members, slots = states[0].shape[1], tables[-1].shape[1]
    scalar = pl.BlockSpec(memory_space=pltpu.SMEM)
    whole = pl.BlockSpec(memory_space=pltpu.VMEM)
    return pl.pallas_call(
        functools.partial(bin_kernel, owned),
        in_specs=[scalar] * 4 + [whole] * 4,
        out_specs=whole,
        out_shape=pltpu.VMEM((receivers.shape[0], owned, members), jnp.float32),
        scratch_shapes=[pltpu.VMEM((2, slots // 8, 8, members), jnp.float32)],
        compiler_params=pltpu.CompilerParams(vmem_limit_bytes=14 * 2**20),
        cost_estimate=pl.CostEstimate(
            flops=10**9, bytes_accessed=30 * 2**20, transcendentals=0
        ),
    )(receivers, *tables, *states)


def factor_kernel(root_scale, products, high, low):
    size = products.shape[1]
    lane = lax.broadcasted_iota(jnp.int32, (size, size), 1)
    line = lax.broadcasted_iota(jnp.int32, (size, size), 0)
    eye = jnp.where(lane == line, 1.0, 0.0)
    left, right = products[:size, :] + eye, eye
    width = 4
    done_left, done_right = [], []
    for start in range(0, size, width):
        top = start % 8
        columns = [
            jnp.broadcast_to(left[:, start + a : start + a + 1], left.shape) for a in range(width)
        ]
        pivots = [[columns[b][top + a : top + a + 1, :] for b in range(width)] for a in range(width)]
        upper = [[None] * width for _ in range(width)]
        inverse = []
        for a in range(width):
            lower = []
            for k in range(a):
                value = pivots[a][k]
                for m in range(k):
                    value = value - lower[m] * upper[m][k]
                lower.append(value * inverse[k])
            for b in range(a, width):
                value = pivots[a][b]
                for m in range(a):
                    value = value - lower[m] * upper[m][b]
                upper[a][b] = value
            inverse.append(1.0 / upper[a][a])
        below = line[: left.shape[0]]
        multipliers = []
        for a in range(width):
            value = columns[a]
            for m in range(a):
                value = value - multipliers[m] * upper[m][a]
            value = value * inverse[a]
            multipliers.append(jnp.where(below > top + a, value, 0.0))
        rows_left, rows_right = [], []
        for a in range(width):
            row_left = left[top + a : top + a + 1, :]
            row_right = right[top + a : top + a + 1, :]
            for m in range(a):
                scale = multipliers[m][top + a : top + a + 1, :]
                row_left = row_left - scale * rows_left[m]
                row_right = row_right - scale * rows_right[m]
            rows_left.append(row_left)
            rows_right.append(row_right)
        for m in range(width):
            left = left - multipliers[m] * rows_left[m]
            right = right - multipliers[m] * rows_right[m]
        if top + width == 8:
            done_left.append(left[:8])
            done_right.append(right[:8])
            left, right = left[8:], right[8:]
    left = jnp.concatenate(done_left, axis=0)
    right = jnp.concatenate(done_right, axis=0)
    pivot = jnp.sum(jnp.where(lane == line, left, 0.0), axis=1, keepdims=True)
    inverse = right * lax.rsqrt(pivot)
    push = products[size : size + 1, :]
    pushed = jnp.sum(inverse * push, axis=1, keepdims=True)
    offset = jnp.sum(inverse * pushed, axis=0, keepdims=True) * (1.0 / root_scale)
    weights = inverse + offset
    weights = weights - jnp.mean(weights, axis=1, keepdims=True) + 1.0 / size
    top_half = weights.astype(jnp.bfloat16)
    high[...] = top_half
    low[...] = (weights - top_half.astype(jnp.float32)).astype(jnp.bfloat16)


def transposed_weights(products, root_scale):
    size = products.shape[1]
    whole = pl.BlockSpec(memory_space=pltpu.VMEM)
    return pl.pallas_call(
        functools.partial(factor_kernel, root_scale),
        in_specs=[whole],
        out_specs=[whole] * 2,
        out_shape=[pltpu.VMEM((size, size), jnp.bfloat16)] * 2,
    )(products)


def analysis_kernel(high, low, state, observed, out, out_observed):
    def update(value):
        near = value.astype(jnp.bfloat16)
        rest = (value - near.astype(jnp.float32)).astype(jnp.bfloat16)

        def times(a, b):
            return lax.dot_general(
                a, b[...], (((1,), (1,)), ((), ())), preferred_element_type=jnp.float32
            )

        return times(near, high) + (times(rest, high) + times(near, low))

    size = out.shape[0]
    start = pl.multiple_of(pl.program_id(0) * size, size)
    out[...] = update(state[pl.ds(start, size), :])

    @pl.when(pl.program_id(0) == 0)
    def _():
        out_observed[...] = update(observed[...])


def analyse(high, low, state, observed):
    rows, members = state.shape
    size = rows // 8
    whole = pl.BlockSpec(memory_space=pltpu.VMEM)
    block = pl.BlockSpec((size, members), lambda k: (k, 0))
    return pl.pallas_call(
        analysis_kernel,
        grid=(rows // size,),
        in_specs=[whole] * 4,
        out_specs=[block, pl.BlockSpec(observed.shape, lambda k: (0, 0))],
        out_shape=[
            jax.ShapeDtypeStruct(state.shape, jnp.float32),
            jax.ShapeDtypeStruct(observed.shape, jnp.float32),
        ],
        compiler_params=pltpu.CompilerParams(vmem_limit_bytes=16 * 2**20),
    )(high, low, state, observed)


def stage_entries(count):
    entries = [(count // 2, 0)]
    for distance in range(count // 2 - 1, 0, -1):
        entries += [(distance, 0), (distance, 1)]
    return entries + [(0, 0)]


def stage(held, axis):
    count = lax.axis_size(axis)
    moving = onward((yield held[0]), axis)
    for distance in range(count // 2 - 1, 0, -1):
        start = 2 * (count // 2 - 1 - distance) + 1
        pair = held[start : start + 2]
        if distance == count // 2 - 1:
            pair = jnp.stack([pair[0] + moving, pair[1]])
        else:
            pair = pair + moving
        moving = onward((yield pair), axis)
    return moving[0] + held[-1], moving[1]


def reduce_to_owner(blocks, first_axis, second_axis):
    count = lax.axis_size(second_axis)
    mine, others = yield from stage(
        blocks.reshape((-1, count) + blocks.shape[1:]), first_axis
    )
    keep, give = [], []
    for distance, whose in stage_entries(count):
        keep.append((mine, others)[whose][distance])
        give.append((others, mine)[whose][-distance % count])
    held = jnp.stack(keep) + swap((yield jnp.stack(give)))
    mine, others = yield from stage(held, second_axis)
    return mine + swap((yield others))


def reduce_together(ahead, behind, ties):
    runs = [ahead, behind]
    pending, done, results = [next(ahead), next(behind)], [0, 0], [None, None]

    def send(k):
        try:
            pending[k] = runs[k].send(pending[k])
            done[k] += 1
        except StopIteration as stop:
            pending[k], results[k] = None, stop.value

    for i, j in ties:
        while done[0] < i:
            send(0)
        while done[1] < j:
            send(1)
        pending[0], pending[1] = lax.optimization_barrier((pending[0], pending[1]))
        send(0)
        send(1)
    for k in range(2):
        while pending[k] is not None:
            send(k)
    return results


def receiver_list(first_axis, second_axis):
    core = lax.axis_index("core")
    direction = 1 - 2 * core
    at = {name: lax.axis_index(name) for name in COL}
    size = {name: lax.axis_size(name) for name in COL}
    entries = stage_entries(size[first_axis])
    count = size[second_axis]
    ahead = np.repeat([entry[0] for entry in entries], count)
    whose = np.repeat([entry[1] for entry in entries], count)
    along = np.tile(np.arange(count), len(entries))
    place = {
        first_axis: (at[first_axis] + direction * ahead) % size[first_axis],
        second_axis: (at[second_axis] + direction * along) % size[second_axis],
    }
    chip = place["z"] * size["x"] + place["x"]
    return (chip * size["core"] + (core + whose) % 2).astype(jnp.int32)


def member_products(observed, value, error, root_scale):
    mean = jnp.mean(observed, axis=1)
    scaled = (observed - mean[:, None]) / (error[:, None] * root_scale)
    innovation = (value - mean) / error
    padding = jnp.zeros((scaled.shape[0], 15), jnp.float32)
    left = jnp.concatenate([scaled, innovation[:, None], padding], axis=1)
    return jnp.dot(left.T, scaled, precision=exact_mode)


def spread_sum(value, axis):
    count = lax.axis_size(axis)
    copies = jnp.broadcast_to(value[None], (count,) + value.shape)
    return jnp.sum(lax.all_to_all(copies, axis, split_axis=0, concat_axis=0, tiled=True), axis=0)


def sum_everywhere(value):
    core = lax.axis_index("core")
    rows = value.shape[0] // 2
    value = value + shift(value, "core", 1)
    part = lax.dynamic_slice_in_dim(value, core * rows, rows, 0)
    for axis in ("x", "lat", "z"):
        part = spread_sum(part, axis)
    other = shift(part, "core", 1)
    return jnp.where(
        core == 0, jnp.concatenate([part, other]), jnp.concatenate([other, part])
    )


def on_device(
    control,
    perturbations,
    zonal_flow,
    meridional_flow,
    diffusivity,
    send_cell,
    send_station,
    send_weight,
    send_count,
    obs_value,
    obs_error,
):
    member_count = perturbations.shape[2]
    step_total, owned_count = obs_value.shape
    fields = (control, zonal_flow, meridional_flow, diffusivity)

    sides = neighbours(*ends_of(perturbations, control))
    tables = [
        jnp.concatenate([table[0, 0], swap(table[0, 0])], axis=0).reshape(-1)
        for table in (send_cell, send_weight, send_count)
    ]
    tables += [send_station[0, 0], swap(send_station[0, 0])]
    first = advance(True, fields, perturbations)
    first, tables, sides = lax.optimization_barrier((first, tables, sides))
    first = with_border(fields, first, sides)
    flat_first = first.reshape(-1, member_count)
    pair_first = swap(flat_first)
    sides = neighbours(*ends_of(first))
    second = with_border(fields, advance(False, fields, first), sides)
    flat_second = second.reshape(-1, member_count)
    pair_second = swap(flat_second)

    root_scale = math.sqrt(member_count - 1.0)
    blocks = bin_rows(receiver_list("x", "z"), tables, (flat_first, pair_first), owned_count)
    first_run = reduce_to_owner(blocks, "x", "z")
    blocks = bin_rows(receiver_list("z", "x"), tables, (flat_second, pair_second), owned_count)
    second_run = reduce_to_owner(blocks, "z", "x")
    observed_first, observed_second = reduce_together(
        first_run, second_run, ((1, 0), (3, 2), (4, 3), (6, 5), (7, 6))
    )
    products = member_products(observed_first, obs_value[0], obs_error[0], root_scale)
    products = products + member_products(
        observed_second, obs_value[1], obs_error[1], root_scale
    )
    high, low = transposed_weights(sum_everywhere(products), root_scale)
    observed = jnp.concatenate([observed_first, observed_second], axis=0)
    analysis, obs_analysis = analyse(high, low, flat_second, observed)
    return (
        analysis.reshape(perturbations.shape),
        obs_analysis.reshape(step_total, owned_count, member_count),
    )


def solution(mesh):
    sizes = (mesh.shape["lat"], mesh.shape["col"] // 8, 4, 2)
    fine = Mesh(mesh.devices.reshape(sizes), ("lat",) + COL)
    grid = P("lat", COL)
    return jax.shard_map(
        on_device,
        mesh=fine,
        in_specs=(
            grid,
            P("lat", COL, None),
            grid,
            grid,
            grid,
            P("lat", COL, None, None),
            P("lat", COL, None, None),
            P("lat", COL, None, None),
            P("lat", COL, None),
            P(None, ("lat",) + COL),
            P(None, ("lat",) + COL),
        ),
        out_specs=(P("lat", COL, None), P(None, ("lat",) + COL, None)),
        check_vma=False,
    )
```

```python
import functools
import math

import jax
import jax.numpy as jnp
from jax import lax
from jax.experimental import pallas as pl
from jax.experimental.pallas import tpu as pltpu
from jax.sharding import Mesh
from jax.sharding import PartitionSpec as P

exact_mode = lax.Precision.HIGHEST
COL = ("z", "x", "core")
UNROLL = 16


def shift(value, axis, step):
    count = lax.axis_size(axis)
    return lax.ppermute(value, axis, [(i, (i + step) % count) for i in range(count)])


def edges(block, offset=None):
    sides = []
    for axis, dim in (("lat", 0), (COL, 1)):
        names = axis if isinstance(axis, tuple) else (axis,)
        count = math.prod(lax.axis_size(name) for name in names)
        forward = [(i, i + 1) for i in range(count - 1)]
        backward = [(target, source) for source, target in forward]
        last = lax.slice_in_dim(block, block.shape[dim] - 1, None, axis=dim)
        first = lax.slice_in_dim(block, 0, 1, axis=dim)
        if offset is not None:
            count = offset.shape[dim]
            last = last + lax.slice_in_dim(offset, count - 1, None, axis=dim)[:, :, None]
            first = first + lax.slice_in_dim(offset, 0, 1, axis=dim)[:, :, None]
        sides.append(lax.ppermute(last, axis, forward))
        sides.append(lax.ppermute(first, axis, backward))
    return sides


def advance_kernel(adds, rates, block, above, below, left, right, out, padded, turned):
    rows, cells, members = block.shape
    groups, lanes = rates.shape[0], rates.shape[1]
    per_group = rows // groups
    for group in range(groups):
        turned[group] = jnp.transpose(rates[group])
    padded[0, 8 : 8 + cells, :] = above[0]
    padded[rows + 1, 8 : 8 + cells, :] = below[0]

    def rate(i, kind):
        lane = (i % per_group) * (lanes // per_group) + kind
        index = jnp.full((cells, members), lane, jnp.int32)
        return jnp.take_along_axis(turned[i // per_group], index, axis=1)

    def fill(i, carry):
        value = block[i]
        padded[i + 1, 8 : 8 + cells, :] = value + rate(i, 4) if adds else value
        padded[i + 1, 7:8, :] = left[i]
        padded[i + 1, 8 + cells : 9 + cells, :] = right[i]
        return carry

    lax.fori_loop(0, rows, fill, 0)

    def row(i, carry):
        centre = padded[i + 1, 8 : 8 + cells, :]
        result = centre + rate(i, 0) * (padded[i + 2, 8 : 8 + cells, :] - centre)
        result = result + rate(i, 1) * (padded[i, 8 : 8 + cells, :] - centre)
        result = result + rate(i, 2) * (padded[i + 1, 9 : 9 + cells, :] - centre)
        out[i] = result + rate(i, 3) * (padded[i + 1, 7 : 7 + cells, :] - centre)
        return carry

    lax.fori_loop(0, rows, row, 0)


def advance(adds, rates, block, sides):
    rows, cells, members = block.shape
    whole = pl.BlockSpec(memory_space=pltpu.VMEM)
    return pl.pallas_call(
        functools.partial(advance_kernel, adds),
        in_specs=[whole] * 6,
        out_specs=whole,
        out_shape=pltpu.VMEM(block.shape, jnp.float32),
        scratch_shapes=[
            pltpu.VMEM((rows + 2, cells + 16, members), jnp.float32),
            pltpu.VMEM((rates.shape[0], cells, rates.shape[1]), jnp.float32),
        ],
        compiler_params=pltpu.CompilerParams(vmem_limit_bytes=24 * 2**20),
        cost_estimate=pl.CostEstimate(
            flops=12 * block.size, bytes_accessed=8 * block.size, transcendentals=0
        ),
    )(rates, block, *sides)


def receiver_of(step, place, size_z, size_x):
    ahead_z, ahead_x = step // size_x, step % size_x
    return ((place[0] + ahead_z) % size_z) * size_x + (place[1] + ahead_x) % size_x


def pick_rows(out, entry, slots, cell, weight, count, states):
    def pick(group, carry):
        for j in range(UNROLL):
            slot = entry * slots + group * UNROLL + j
            row, factor = cell[slot], weight[slot]
            tile, line = group * (UNROLL // 8) + j // 8, j % 8
            for k in range(2):
                out[k, tile, line : line + 1, :] = states[k][pl.ds(row, 1), :] * factor
        return carry

    lax.fori_loop(0, (count[entry] + UNROLL - 1) // UNROLL, pick, 0)


def own_kernel(size_z, size_x, place, cell, weight, count, first, second, out):
    slots = 8 * out.shape[2]

    def one(step, carry):
        out[step] = jnp.zeros(out.shape[1:], jnp.float32)
        receiver = receiver_of(step, place, size_z, size_x)
        pick_rows(out.at[step], receiver, slots, cell, weight, count, (first, second))
        return carry

    lax.fori_loop(0, out.shape[0], one, 0)


def bin_kernel(
    size_z, size_x, owned, place, cell, weight, count, station, held, first, second, *rest
):
    out_a, out_b, picked = rest
    width = out_a.shape[3]
    cut = out_a.shape[2] - owned
    receivers, slots = size_z * size_x, station.shape[1]
    picked[...] = jnp.zeros_like(picked)
    own = lax.broadcasted_iota(jnp.int32, (owned, slots), 0)

    def one(step, carry):
        receiver = receiver_of(step, place, size_z, size_x)
        pick_rows(picked, receivers + receiver, slots, cell, weight, count, (first, second))
        hots = []
        for e in range(2):
            hit = station[pl.ds(e * receivers + receiver, 1), :] == own
            hots.append(jnp.where(hit, 1.0, 0.0).astype(jnp.bfloat16))
        rows = [[held[step, k].reshape(slots, width) for k in range(2)]]
        rows.append([picked[k].reshape(slots, width) for k in range(2)])
        value = jnp.concatenate([jnp.concatenate(pair, axis=1) for pair in rows], axis=0)
        high = value.astype(jnp.bfloat16)
        low = (value - high.astype(jnp.float32)).astype(jnp.bfloat16)
        total = jnp.dot(
            jnp.concatenate(hots + hots, axis=1),
            jnp.concatenate([high, low], axis=0),
            preferred_element_type=jnp.float32,
        )
        ahead_z, ahead_x = step // size_x, step % size_x
        out_a[ahead_x, ahead_z, :owned, :] = total[:, :width]
        out_a[ahead_x, ahead_z, owned:, :] = total[:cut, width:]
        out_b[ahead_z, ahead_x] = total[cut:, width:]
        return carry

    lax.fori_loop(0, receivers, one, 0)


def bin_rows(place, cell, weight, count, station, states, owned):
    size_z, size_x = lax.axis_size("z"), lax.axis_size("x")
    members, slots = states[0].shape[1], station.shape[1]
    rows_a = owned + owned // 8
    rows_b = 2 * owned - rows_a
    scalar = pl.BlockSpec(memory_space=pltpu.SMEM)
    whole = pl.BlockSpec(memory_space=pltpu.VMEM)
    held = pl.pallas_call(
        functools.partial(own_kernel, size_z, size_x),
        in_specs=[scalar] * 4 + [whole] * 2,
        out_specs=whole,
        out_shape=pltpu.VMEM((size_z * size_x, 2, slots // 8, 8, members), jnp.float32),
        compiler_params=pltpu.CompilerParams(vmem_limit_bytes=24 * 2**20),
        cost_estimate=pl.CostEstimate(
            flops=10**8, bytes_accessed=20 * 2**20, transcendentals=0
        ),
    )(place, cell, weight, count, *states[:2])
    return pl.pallas_call(
        functools.partial(bin_kernel, size_z, size_x, owned),
        in_specs=[scalar] * 4 + [whole] * 4,
        out_specs=[whole] * 2,
        out_shape=[
            pltpu.VMEM((size_x, size_z, rows_a, members), jnp.float32),
            pltpu.VMEM((size_z, size_x, rows_b, members), jnp.float32),
        ],
        scratch_shapes=[pltpu.VMEM((2, slots // 8, 8, members), jnp.float32)],
        compiler_params=pltpu.CompilerParams(vmem_limit_bytes=32 * 2**20),
        cost_estimate=pl.CostEstimate(flops=10**9, bytes_accessed=30 * 2**20, transcendentals=0),
    )(place, cell, weight, count, station, held, *states[2:])


def factor_kernel(root_scale, products, high, low):
    size = products.shape[1]
    lane = lax.broadcasted_iota(jnp.int32, (size, size), 1)
    line = lax.broadcasted_iota(jnp.int32, (size, size), 0)
    eye = jnp.where(lane == line, 1.0, 0.0)
    left, right = products[:size, :] + eye, eye
    width = 4
    done_left, done_right = [], []
    for start in range(0, size, width):
        top = start % 8
        columns = [
            jnp.broadcast_to(left[:, start + a : start + a + 1], left.shape) for a in range(width)
        ]
        pivots = [[columns[b][top + a : top + a + 1, :] for b in range(width)] for a in range(width)]
        upper = [[None] * width for _ in range(width)]
        inverse = []
        for a in range(width):
            lower = []
            for k in range(a):
                value = pivots[a][k]
                for m in range(k):
                    value = value - lower[m] * upper[m][k]
                lower.append(value * inverse[k])
            for b in range(a, width):
                value = pivots[a][b]
                for m in range(a):
                    value = value - lower[m] * upper[m][b]
                upper[a][b] = value
            inverse.append(1.0 / upper[a][a])
        below = line[: left.shape[0]]
        multipliers = []
        for a in range(width):
            value = columns[a]
            for m in range(a):
                value = value - multipliers[m] * upper[m][a]
            value = value * inverse[a]
            multipliers.append(jnp.where(below > top + a, value, 0.0))
        rows_left, rows_right = [], []
        for a in range(width):
            row_left = left[top + a : top + a + 1, :]
            row_right = right[top + a : top + a + 1, :]
            for m in range(a):
                scale = multipliers[m][top + a : top + a + 1, :]
                row_left = row_left - scale * rows_left[m]
                row_right = row_right - scale * rows_right[m]
            rows_left.append(row_left)
            rows_right.append(row_right)
        for m in range(width):
            left = left - multipliers[m] * rows_left[m]
            right = right - multipliers[m] * rows_right[m]
        if top + width == 8:
            done_left.append(left[:8])
            done_right.append(right[:8])
            left, right = left[8:], right[8:]
    left = jnp.concatenate(done_left, axis=0)
    right = jnp.concatenate(done_right, axis=0)
    pivot = jnp.sum(jnp.where(lane == line, left, 0.0), axis=1, keepdims=True)
    inverse = right * lax.rsqrt(pivot)
    push = products[size : size + 1, :]
    pushed = jnp.sum(inverse * push, axis=1, keepdims=True)
    offset = jnp.sum(inverse * pushed, axis=0, keepdims=True) * (1.0 / root_scale)
    weights = inverse + offset
    weights = weights - jnp.mean(weights, axis=1, keepdims=True) + 1.0 / size
    top_half = weights.astype(jnp.bfloat16)
    high[...] = top_half
    low[...] = (weights - top_half.astype(jnp.float32)).astype(jnp.bfloat16)


def transposed_weights(products, root_scale):
    size = products.shape[1]
    whole = pl.BlockSpec(memory_space=pltpu.VMEM)
    return pl.pallas_call(
        functools.partial(factor_kernel, root_scale),
        in_specs=[whole],
        out_specs=[whole] * 2,
        out_shape=[pltpu.VMEM((size, size), jnp.bfloat16)] * 2,
    )(products)


def analysis_kernel(high, low, state, observed, out, out_observed):
    def update(value):
        near = value.astype(jnp.bfloat16)
        rest = (value - near.astype(jnp.float32)).astype(jnp.bfloat16)

        def times(a, b):
            return lax.dot_general(
                a, b[...], (((1,), (1,)), ((), ())), preferred_element_type=jnp.float32
            )

        return times(near, high) + (times(rest, high) + times(near, low))

    out[...] = update(state[...])

    @pl.when(pl.program_id(0) == 0)
    def _():
        out_observed[...] = update(observed[...])


def analyse(high, low, state, observed):
    rows, members = state.shape
    whole = pl.BlockSpec(memory_space=pltpu.VMEM)
    block = pl.BlockSpec((rows // 8, members), lambda k: (k, 0))
    return pl.pallas_call(
        analysis_kernel,
        grid=(8,),
        in_specs=[whole, whole, block, whole],
        out_specs=[block, pl.BlockSpec(observed.shape, lambda k: (0, 0))],
        out_shape=[
            jax.ShapeDtypeStruct(state.shape, jnp.float32),
            jax.ShapeDtypeStruct(observed.shape, jnp.float32),
        ],
    )(high, low, state, observed)


def ring_reduce(blocks, axis):
    count = len(blocks)
    half = count // 2
    cut = blocks[half].shape[-2] // 2
    up = shift(blocks[half][..., :cut, :], axis, 1)
    down = shift(blocks[half][..., cut:, :], axis, -1)
    ahead, behind = blocks[half - 1], blocks[count - half + 1]
    up = jnp.concatenate([ahead[..., :cut, :] + up, ahead[..., cut:, :]], axis=-2)
    down = jnp.concatenate([behind[..., :cut, :], behind[..., cut:, :] + down], axis=-2)
    for k in range(half - 1, 0, -1):
        up = shift(up, axis, 1)
        down = shift(down, axis, -1)
        if k > 1:
            up = blocks[k - 1] + up
            down = blocks[count - k + 1] + down
    return blocks[0] + up + down


def reduce_to_owner(block_a, block_b):
    size_x, size_z = block_a.shape[:2]
    part_a = ring_reduce([block_a[k] for k in range(size_x)], "x")
    part_b = ring_reduce([block_b[k] for k in range(size_z)], "z")
    part_a = ring_reduce([part_a[k] for k in range(size_z)], "z")
    part_b = ring_reduce([part_b[k] for k in range(size_x)], "x")
    return jnp.concatenate([part_a, part_b], axis=0)


def spread_sum(value, axis):
    count = lax.axis_size(axis)
    copies = jnp.broadcast_to(value[None], (count,) + value.shape)
    return jnp.sum(lax.all_to_all(copies, axis, split_axis=0, concat_axis=0, tiled=True), axis=0)


def sum_everywhere(value):
    core = lax.axis_index("core")
    rows = value.shape[0] // 2
    value = value + shift(value, "core", 1)
    part = lax.dynamic_slice_in_dim(value, core * rows, rows, 0)
    for axis in ("x", "lat", "z"):
        part = spread_sum(part, axis)
    other = shift(part, "core", 1)
    return jnp.where(
        core == 0, jnp.concatenate([part, other]), jnp.concatenate([other, part])
    )


def on_device(
    control,
    perturbations,
    zonal_flow,
    meridional_flow,
    diffusivity,
    send_cell,
    send_station,
    send_weight,
    send_count,
    obs_value,
    obs_error,
):
    member_count = perturbations.shape[2]
    step_total, owned_count = obs_value.shape
    slots = send_cell.shape[3]
    size_z, size_x, size_c = (lax.axis_size(name) for name in COL)
    core = lax.axis_index("core")
    place = jnp.stack([lax.axis_index("z"), lax.axis_index("x")]).astype(jnp.int32)

    live = lax.broadcasted_iota(jnp.int32, send_cell.shape[2:], 1) < send_count[0, 0][:, None]
    station_live = jnp.where(live, send_station[0, 0], -1)
    whole_tables = jnp.concatenate(
        [
            send_cell[0, 0],
            station_live,
            jnp.broadcast_to(send_count[0, 0][:, None], (send_cell.shape[2], slots)),
        ],
        axis=1,
    ).reshape(size_z * size_x, size_c, 3 * slots)
    whole_weights = send_weight[0, 0].reshape(size_z * size_x, size_c, slots)
    index_own = lax.dynamic_index_in_dim(whole_tables, core, 1, keepdims=False)
    index_pair = shift(
        lax.dynamic_index_in_dim(whole_tables, 1 - core, 1, keepdims=False), "core", 1
    )
    weight_own = lax.dynamic_index_in_dim(whole_weights, core, 1, keepdims=False)
    weight_pair = shift(
        lax.dynamic_index_in_dim(whole_weights, 1 - core, 1, keepdims=False), "core", 1
    )

    zero = jnp.zeros_like(control)
    rates = jnp.stack(
        [
            diffusivity + jnp.maximum(-zonal_flow, 0.0),
            diffusivity + jnp.maximum(zonal_flow, 0.0),
            diffusivity + jnp.maximum(-meridional_flow, 0.0),
            diffusivity + jnp.maximum(meridional_flow, 0.0),
            control,
            zero,
            zero,
            zero,
        ],
        axis=1,
    ).reshape(-1, member_count, control.shape[1])
    first = advance(True, rates, perturbations, edges(perturbations, control))
    index = jnp.concatenate([index_own, index_pair], axis=0)
    weight = jnp.concatenate([weight_own, weight_pair], axis=0)
    tables = (
        index[:, :slots].reshape(-1),
        weight.reshape(-1),
        index[:, 2 * slots],
        index[:, slots : 2 * slots],
    )
    sides, tables = lax.optimization_barrier((edges(first), tables))
    second = advance(False, rates, first, sides)
    flat = [state.reshape(-1, member_count) for state in (first, second)]
    paired = [shift(state, "core", 1) for state in flat]
    blocks = bin_rows(place, *tables, flat + paired, owned_count)
    observed = reduce_to_owner(*blocks).reshape(step_total, owned_count, member_count)

    root_scale = math.sqrt(member_count - 1.0)
    obs_mean = jnp.mean(observed, axis=2)
    spread = observed - obs_mean[:, :, None]
    scaled = (spread / (obs_error[:, :, None] * root_scale)).reshape(-1, member_count)
    innovation = ((obs_value - obs_mean) / obs_error).reshape(-1)
    products = jnp.dot(
        jnp.concatenate(
            [scaled, innovation[:, None], jnp.zeros((scaled.shape[0], 15), jnp.float32)], axis=1
        ).T,
        scaled,
        precision=exact_mode,
    )
    products = sum_everywhere(products)
    high, low = transposed_weights(products, root_scale)
    analysis, obs_analysis = analyse(
        high, low, flat[-1], observed.reshape(-1, member_count)
    )
    return (analysis.reshape(perturbations.shape), obs_analysis.reshape(observed.shape))


def solution(mesh):
    sizes = (mesh.shape["lat"], mesh.shape["col"] // 8, 4, 2)
    fine = Mesh(mesh.devices.reshape(sizes), ("lat",) + COL)
    grid = P("lat", COL)
    return jax.shard_map(
        on_device,
        mesh=fine,
        in_specs=(
            grid,
            P("lat", COL, None),
            grid,
            grid,
            grid,
            P("lat", COL, None, None),
            P("lat", COL, None, None),
            P("lat", COL, None, None),
            P("lat", COL, None),
            P(None, ("lat",) + COL),
            P(None, ("lat",) + COL),
        ),
        out_specs=(P("lat", COL, None), P(None, ("lat",) + COL, None)),
        check_vma=False,
    )
```

```python
import functools
import math

import jax
import jax.numpy as jnp
from jax import lax
from jax.experimental import pallas as pl
from jax.experimental.pallas import tpu as pltpu
from jax.sharding import Mesh
from jax.sharding import PartitionSpec as P

exact_mode = lax.Precision.HIGHEST
COL = ("z", "x", "core")
UNROLL = 16


def shift(value, axis, step):
    count = lax.axis_size(axis)
    return lax.ppermute(value, axis, [(i, (i + step) % count) for i in range(count)])


def ends_of(block, offset=None):
    parts = []
    for dim in (0, 1):
        for start in (block.shape[dim] - 1, 0):
            part = lax.slice_in_dim(block, start, start + 1, axis=dim)
            if offset is not None:
                part = part + lax.slice_in_dim(offset, start, start + 1, axis=dim)[:, :, None]
            parts.append(part)
    return parts


def edges(parts):
    sides = []
    for axis, (last, first) in (("lat", parts[:2]), (COL, parts[2:])):
        names = axis if isinstance(axis, tuple) else (axis,)
        count = math.prod(lax.axis_size(name) for name in names)
        forward = [(i, i + 1) for i in range(count - 1)]
        backward = [(target, source) for source, target in forward]
        sides.append(lax.ppermute(last, axis, forward))
        sides.append(lax.ppermute(first, axis, backward))
    return sides


def advance_kernel(adds, rates, block, above, below, left, right, out, padded, turned):
    rows, cells, members = block.shape
    groups, lanes = rates.shape[0], rates.shape[1]
    per_group = rows // groups
    for group in range(groups):
        turned[group] = jnp.transpose(rates[group])
    padded[0, 8 : 8 + cells, :] = above[0]
    padded[rows + 1, 8 : 8 + cells, :] = below[0]

    def rate(i, kind):
        lane = (i % per_group) * (lanes // per_group) + kind
        index = jnp.full((cells, members), lane, jnp.int32)
        return jnp.take_along_axis(turned[i // per_group], index, axis=1)

    def fill(i, carry):
        value = block[i]
        padded[i + 1, 8 : 8 + cells, :] = value + rate(i, 4) if adds else value
        padded[i + 1, 7:8, :] = left[i]
        padded[i + 1, 8 + cells : 9 + cells, :] = right[i]
        return carry

    lax.fori_loop(0, rows, fill, 0)

    def row(i, carry):
        centre = padded[i + 1, 8 : 8 + cells, :]
        result = centre + rate(i, 0) * (padded[i + 2, 8 : 8 + cells, :] - centre)
        result = result + rate(i, 1) * (padded[i, 8 : 8 + cells, :] - centre)
        result = result + rate(i, 2) * (padded[i + 1, 9 : 9 + cells, :] - centre)
        out[i] = result + rate(i, 3) * (padded[i + 1, 7 : 7 + cells, :] - centre)
        return carry

    lax.fori_loop(0, rows, row, 0)


def advance(adds, rates, block, sides):
    rows, cells, members = block.shape
    whole = pl.BlockSpec(memory_space=pltpu.VMEM)
    return pl.pallas_call(
        functools.partial(advance_kernel, adds),
        in_specs=[whole] * 6,
        out_specs=whole,
        out_shape=pltpu.VMEM(block.shape, jnp.float32),
        scratch_shapes=[
            pltpu.VMEM((rows + 2, cells + 16, members), jnp.float32),
            pltpu.VMEM((rates.shape[0], cells, rates.shape[1]), jnp.float32),
        ],
        compiler_params=pltpu.CompilerParams(vmem_limit_bytes=24 * 2**20),
        cost_estimate=pl.CostEstimate(
            flops=12 * block.size, bytes_accessed=8 * block.size, transcendentals=0
        ),
    )(rates, block, *sides)


def receiver_of(step, place, size_z, size_x):
    ahead_z, ahead_x = step // size_x, step % size_x
    chip = ((place[0] + ahead_z) % size_z) * size_x + (place[1] + ahead_x) % size_x
    return 2 * chip + place[2]


def pick_rows(out, entry, slots, cell, weight, count, states):
    def pick(group, carry):
        for j in range(UNROLL):
            slot = entry * slots + group * UNROLL + j
            row, factor = cell[slot], weight[slot]
            tile, line = group * (UNROLL // 8) + j // 8, j % 8
            for k in range(2):
                out[k, tile, line : line + 1, :] = states[k][pl.ds(row, 1), :] * factor
        return carry

    lax.fori_loop(0, (count[entry] + UNROLL - 1) // UNROLL, pick, 0)


def own_kernel(size_z, size_x, place, cell, weight, count, first, second, out):
    slots = 8 * out.shape[2]

    def one(step, carry):
        out[step] = jnp.zeros(out.shape[1:], jnp.float32)
        receiver = receiver_of(step, place, size_z, size_x)
        pick_rows(out.at[step], receiver, slots, cell, weight, count, (first, second))
        return carry

    lax.fori_loop(0, out.shape[0], one, 0)


def bin_kernel(
    size_z, size_x, owned, place, cell, weight, count, station_own, station_pair, held, first, second, *rest
):
    out_a, out_b, picked = rest
    width = out_a.shape[3]
    cut = out_a.shape[2] - owned
    receivers, slots = station_own.shape
    order = lax.broadcasted_iota(jnp.int32, (1, slots), 1)
    picked[...] = jnp.zeros_like(picked)
    own = lax.broadcasted_iota(jnp.int32, (owned, slots), 0)

    def one(step, carry):
        receiver = receiver_of(step, place, size_z, size_x)
        pick_rows(picked, receivers + receiver, slots, cell, weight, count, (first, second))
        hots = []
        for e in range(2):
            station = (station_own, station_pair)[e][pl.ds(receiver, 1), :]
            live = order < count[e * receivers + receiver]
            hit = jnp.where(live, station, -1) == own
            hots.append(jnp.where(hit, 1.0, 0.0).astype(jnp.bfloat16))
        rows = [[held[step, k].reshape(slots, width) for k in range(2)]]
        rows.append([picked[k].reshape(slots, width) for k in range(2)])
        value = jnp.concatenate([jnp.concatenate(pair, axis=1) for pair in rows], axis=0)
        high = value.astype(jnp.bfloat16)
        low = (value - high.astype(jnp.float32)).astype(jnp.bfloat16)
        total = jnp.dot(
            jnp.concatenate(hots + hots, axis=1),
            jnp.concatenate([high, low], axis=0),
            preferred_element_type=jnp.float32,
        )
        ahead_z, ahead_x = step // size_x, step % size_x
        out_a[ahead_x, ahead_z, :owned, :] = total[:, :width]
        out_a[ahead_x, ahead_z, owned:, :] = total[:cut, width:]
        out_b[ahead_z, ahead_x] = total[cut:, width:]
        return carry

    lax.fori_loop(0, size_z * size_x, one, 0)


def bin_rows(place, cell, weight, count, station_own, station_pair, states, owned):
    size_z, size_x = lax.axis_size("z"), lax.axis_size("x")
    members, slots = states[0].shape[1], station_own.shape[1]
    rows_a = owned + owned // 8
    rows_b = 2 * owned - rows_a
    scalar = pl.BlockSpec(memory_space=pltpu.SMEM)
    whole = pl.BlockSpec(memory_space=pltpu.VMEM)
    held = pl.pallas_call(
        functools.partial(own_kernel, size_z, size_x),
        in_specs=[scalar] * 4 + [whole] * 2,
        out_specs=whole,
        out_shape=pltpu.VMEM((size_z * size_x, 2, slots // 8, 8, members), jnp.float32),
        compiler_params=pltpu.CompilerParams(vmem_limit_bytes=24 * 2**20),
        cost_estimate=pl.CostEstimate(
            flops=10**8, bytes_accessed=20 * 2**20, transcendentals=0
        ),
    )(place, cell, weight, count, *states[:2])
    return pl.pallas_call(
        functools.partial(bin_kernel, size_z, size_x, owned),
        in_specs=[scalar] * 4 + [whole] * 5,
        out_specs=[whole] * 2,
        out_shape=[
            pltpu.VMEM((size_x, size_z, rows_a, members), jnp.float32),
            pltpu.VMEM((size_z, size_x, rows_b, members), jnp.float32),
        ],
        scratch_shapes=[pltpu.VMEM((2, slots // 8, 8, members), jnp.float32)],
        compiler_params=pltpu.CompilerParams(vmem_limit_bytes=32 * 2**20),
        cost_estimate=pl.CostEstimate(flops=10**9, bytes_accessed=30 * 2**20, transcendentals=0),
    )(place, cell, weight, count, station_own, station_pair, held, *states[2:])


def factor_kernel(root_scale, products, high, low):
    size = products.shape[1]
    lane = lax.broadcasted_iota(jnp.int32, (size, size), 1)
    line = lax.broadcasted_iota(jnp.int32, (size, size), 0)
    eye = jnp.where(lane == line, 1.0, 0.0)
    left, right = products[:size, :] + eye, eye
    width = 4
    done_left, done_right = [], []
    for start in range(0, size, width):
        top = start % 8
        columns = [
            jnp.broadcast_to(left[:, start + a : start + a + 1], left.shape) for a in range(width)
        ]
        pivots = [[columns[b][top + a : top + a + 1, :] for b in range(width)] for a in range(width)]
        upper = [[None] * width for _ in range(width)]
        inverse = []
        for a in range(width):
            lower = []
            for k in range(a):
                value = pivots[a][k]
                for m in range(k):
                    value = value - lower[m] * upper[m][k]
                lower.append(value * inverse[k])
            for b in range(a, width):
                value = pivots[a][b]
                for m in range(a):
                    value = value - lower[m] * upper[m][b]
                upper[a][b] = value
            inverse.append(1.0 / upper[a][a])
        below = line[: left.shape[0]]
        multipliers = []
        for a in range(width):
            value = columns[a]
            for m in range(a):
                value = value - multipliers[m] * upper[m][a]
            value = value * inverse[a]
            multipliers.append(jnp.where(below > top + a, value, 0.0))
        rows_left, rows_right = [], []
        for a in range(width):
            row_left = left[top + a : top + a + 1, :]
            row_right = right[top + a : top + a + 1, :]
            for m in range(a):
                scale = multipliers[m][top + a : top + a + 1, :]
                row_left = row_left - scale * rows_left[m]
                row_right = row_right - scale * rows_right[m]
            rows_left.append(row_left)
            rows_right.append(row_right)
        for m in range(width):
            left = left - multipliers[m] * rows_left[m]
            right = right - multipliers[m] * rows_right[m]
        if top + width == 8:
            done_left.append(left[:8])
            done_right.append(right[:8])
            left, right = left[8:], right[8:]
    left = jnp.concatenate(done_left, axis=0)
    right = jnp.concatenate(done_right, axis=0)
    pivot = jnp.sum(jnp.where(lane == line, left, 0.0), axis=1, keepdims=True)
    inverse = right * lax.rsqrt(pivot)
    push = products[size : size + 1, :]
    pushed = jnp.sum(inverse * push, axis=1, keepdims=True)
    offset = jnp.sum(inverse * pushed, axis=0, keepdims=True) * (1.0 / root_scale)
    weights = inverse + offset
    weights = weights - jnp.mean(weights, axis=1, keepdims=True) + 1.0 / size
    top_half = weights.astype(jnp.bfloat16)
    high[...] = top_half
    low[...] = (weights - top_half.astype(jnp.float32)).astype(jnp.bfloat16)


def transposed_weights(products, root_scale):
    size = products.shape[1]
    whole = pl.BlockSpec(memory_space=pltpu.VMEM)
    return pl.pallas_call(
        functools.partial(factor_kernel, root_scale),
        in_specs=[whole],
        out_specs=[whole] * 2,
        out_shape=[pltpu.VMEM((size, size), jnp.bfloat16)] * 2,
    )(products)


def analysis_kernel(high, low, state, observed, out, out_observed):
    def update(value):
        near = value.astype(jnp.bfloat16)
        rest = (value - near.astype(jnp.float32)).astype(jnp.bfloat16)

        def times(a, b):
            return lax.dot_general(
                a, b[...], (((1,), (1,)), ((), ())), preferred_element_type=jnp.float32
            )

        return times(near, high) + (times(rest, high) + times(near, low))

    out[...] = update(state[...])

    @pl.when(pl.program_id(0) == 0)
    def _():
        out_observed[...] = update(observed[...])


def analyse(high, low, state, observed):
    rows, members = state.shape
    whole = pl.BlockSpec(memory_space=pltpu.VMEM)
    block = pl.BlockSpec((rows // 8, members), lambda k: (k, 0))
    return pl.pallas_call(
        analysis_kernel,
        grid=(8,),
        in_specs=[whole, whole, block, whole],
        out_specs=[block, pl.BlockSpec(observed.shape, lambda k: (0, 0))],
        out_shape=[
            jax.ShapeDtypeStruct(state.shape, jnp.float32),
            jax.ShapeDtypeStruct(observed.shape, jnp.float32),
        ],
    )(high, low, state, observed)


def ring_reduce(blocks, axis):
    count = len(blocks)
    half = count // 2
    cut = blocks[half].shape[-2] // 2
    up = shift(blocks[half][..., :cut, :], axis, 1)
    down = shift(blocks[half][..., cut:, :], axis, -1)
    ahead, behind = blocks[half - 1], blocks[count - half + 1]
    up = jnp.concatenate([ahead[..., :cut, :] + up, ahead[..., cut:, :]], axis=-2)
    down = jnp.concatenate([behind[..., :cut, :], behind[..., cut:, :] + down], axis=-2)
    for k in range(half - 1, 0, -1):
        up = shift(up, axis, 1)
        down = shift(down, axis, -1)
        if k > 1:
            up = blocks[k - 1] + up
            down = blocks[count - k + 1] + down
    return blocks[0] + up + down


def reduce_to_owner(block_a, block_b):
    size_x, size_z = block_a.shape[:2]
    part_a = ring_reduce([block_a[k] for k in range(size_x)], "x")
    part_b = ring_reduce([block_b[k] for k in range(size_z)], "z")
    part_a = ring_reduce([part_a[k] for k in range(size_z)], "z")
    part_b = ring_reduce([part_b[k] for k in range(size_x)], "x")
    return jnp.concatenate([part_a, part_b], axis=0)


def spread_sum(value, axis):
    count = math.prod(lax.axis_size(name) for name in axis)
    copies = jnp.broadcast_to(value[None], (count,) + value.shape)
    return jnp.sum(lax.all_to_all(copies, axis, split_axis=0, concat_axis=0, tiled=True), axis=0)


def sum_everywhere(value):
    core = lax.axis_index("core")
    rows = value.shape[0] // 2
    value = value + shift(value, "core", 1)
    part = lax.dynamic_slice_in_dim(value, core * rows, rows, 0)
    for axis in (("lat", "x"), ("z",)):
        part = spread_sum(part, axis)
    other = shift(part, "core", 1)
    return jnp.where(
        core == 0, jnp.concatenate([part, other]), jnp.concatenate([other, part])
    )


def on_device(
    control,
    perturbations,
    zonal_flow,
    meridional_flow,
    diffusivity,
    send_cell,
    send_station,
    send_weight,
    send_count,
    obs_value,
    obs_error,
):
    member_count = perturbations.shape[2]
    step_total, owned_count = obs_value.shape
    place = jnp.stack([lax.axis_index(name) for name in COL]).astype(jnp.int32)
    swapped = [
        shift(table[0, 0], "core", 1)
        for table in (send_cell, send_weight, send_count, send_station)
    ]

    zero = jnp.zeros_like(control)
    rates = jnp.stack(
        [
            diffusivity + jnp.maximum(-zonal_flow, 0.0),
            diffusivity + jnp.maximum(zonal_flow, 0.0),
            diffusivity + jnp.maximum(-meridional_flow, 0.0),
            diffusivity + jnp.maximum(meridional_flow, 0.0),
            control,
            zero,
            zero,
            zero,
        ],
        axis=1,
    ).reshape(-1, member_count, control.shape[1])
    first = advance(True, rates, perturbations, edges(ends_of(perturbations, control)))
    tables = [
        jnp.concatenate([table[0, 0], other], axis=0).reshape(-1)
        for table, other in zip((send_cell, send_weight, send_count), swapped)
    ] + [send_station[0, 0], swapped[3]]
    sides, tables = lax.optimization_barrier((edges(ends_of(first)), tables))
    second = advance(False, rates, first, sides)
    flat = [state.reshape(-1, member_count) for state in (first, second)]
    paired = [shift(state, "core", 1) for state in flat]
    blocks = bin_rows(place, *tables, flat + paired, owned_count)
    observed = reduce_to_owner(*blocks).reshape(step_total, owned_count, member_count)

    root_scale = math.sqrt(member_count - 1.0)
    obs_mean = jnp.mean(observed, axis=2)
    spread = observed - obs_mean[:, :, None]
    scaled = (spread / (obs_error[:, :, None] * root_scale)).reshape(-1, member_count)
    innovation = ((obs_value - obs_mean) / obs_error).reshape(-1)
    products = jnp.dot(
        jnp.concatenate(
            [scaled, innovation[:, None], jnp.zeros((scaled.shape[0], 15), jnp.float32)], axis=1
        ).T,
        scaled,
        precision=exact_mode,
    )
    products = sum_everywhere(products)
    high, low = transposed_weights(products, root_scale)
    analysis, obs_analysis = analyse(
        high, low, flat[-1], observed.reshape(-1, member_count)
    )
    return (analysis.reshape(perturbations.shape), obs_analysis.reshape(observed.shape))


def solution(mesh):
    sizes = (mesh.shape["lat"], mesh.shape["col"] // 8, 4, 2)
    fine = Mesh(mesh.devices.reshape(sizes), ("lat",) + COL)
    grid = P("lat", COL)
    return jax.shard_map(
        on_device,
        mesh=fine,
        in_specs=(
            grid,
            P("lat", COL, None),
            grid,
            grid,
            grid,
            P("lat", COL, None, None),
            P("lat", COL, None, None),
            P("lat", COL, None, None),
            P("lat", COL, None),
            P(None, ("lat",) + COL),
            P(None, ("lat",) + COL),
        ),
        out_specs=(P("lat", COL, None), P(None, ("lat",) + COL, None)),
        check_vma=False,
    )
```

```python
import functools
import math

import jax
import jax.numpy as jnp
from jax import lax
from jax.experimental import pallas as pl
from jax.experimental.pallas import tpu as pltpu
from jax.sharding import Mesh
from jax.sharding import PartitionSpec as P

exact_mode = lax.Precision.HIGHEST
COL = ("z", "x", "core")
UNROLL = 16


def shift(value, axis, step):
    count = lax.axis_size(axis)
    return lax.ppermute(value, axis, [(i, (i + step) % count) for i in range(count)])


def ends_of(block, offset=None):
    parts = []
    for dim in (0, 1):
        for start in (block.shape[dim] - 1, 0):
            part = lax.slice_in_dim(block, start, start + 1, axis=dim)
            if offset is not None:
                part = part + lax.slice_in_dim(offset, start, start + 1, axis=dim)[:, :, None]
            parts.append(part)
    return parts


def edges(parts):
    sides = []
    for axis, (last, first) in (("lat", parts[:2]), (COL, parts[2:])):
        names = axis if isinstance(axis, tuple) else (axis,)
        count = math.prod(lax.axis_size(name) for name in names)
        forward = [(i, i + 1) for i in range(count - 1)]
        backward = [(target, source) for source, target in forward]
        sides.append(lax.ppermute(last, axis, forward))
        sides.append(lax.ppermute(first, axis, backward))
    return sides


def advance_kernel(adds, rates, block, above, below, left, right, out, padded, turned):
    rows, cells, members = block.shape
    groups, lanes = rates.shape[0], rates.shape[1]
    per_group = rows // groups
    for group in range(groups):
        turned[group] = jnp.transpose(rates[group])
    padded[0, 8 : 8 + cells, :] = above[0]
    padded[rows + 1, 8 : 8 + cells, :] = below[0]

    def rate(i, kind):
        lane = (i % per_group) * (lanes // per_group) + kind
        index = jnp.full((cells, members), lane, jnp.int32)
        return jnp.take_along_axis(turned[i // per_group], index, axis=1)

    def fill(i, carry):
        value = block[i]
        padded[i + 1, 8 : 8 + cells, :] = value + rate(i, 4) if adds else value
        padded[i + 1, 7:8, :] = left[i]
        padded[i + 1, 8 + cells : 9 + cells, :] = right[i]
        return carry

    lax.fori_loop(0, rows, fill, 0)

    def row(i, carry):
        centre = padded[i + 1, 8 : 8 + cells, :]
        result = centre + rate(i, 0) * (padded[i + 2, 8 : 8 + cells, :] - centre)
        result = result + rate(i, 1) * (padded[i, 8 : 8 + cells, :] - centre)
        result = result + rate(i, 2) * (padded[i + 1, 9 : 9 + cells, :] - centre)
        out[i] = result + rate(i, 3) * (padded[i + 1, 7 : 7 + cells, :] - centre)
        return carry

    lax.fori_loop(0, rows, row, 0)


def advance(adds, rates, block, sides):
    rows, cells, members = block.shape
    whole = pl.BlockSpec(memory_space=pltpu.VMEM)
    return pl.pallas_call(
        functools.partial(advance_kernel, adds),
        in_specs=[whole] * 6,
        out_specs=whole,
        out_shape=pltpu.VMEM(block.shape, jnp.float32),
        scratch_shapes=[
            pltpu.VMEM((rows + 2, cells + 16, members), jnp.float32),
            pltpu.VMEM((rates.shape[0], cells, rates.shape[1]), jnp.float32),
        ],
        compiler_params=pltpu.CompilerParams(vmem_limit_bytes=24 * 2**20),
        cost_estimate=pl.CostEstimate(
            flops=12 * block.size, bytes_accessed=8 * block.size, transcendentals=0
        ),
    )(rates, block, *sides)


def receiver_of(step, place, size_z, size_x):
    ahead_z, ahead_x = step // size_x, step % size_x
    chip = ((place[0] + ahead_z) % size_z) * size_x + (place[1] + ahead_x) % size_x
    return 2 * chip + place[2]


def pick_rows(out, entry, slots, cell, weight, count, states):
    def pick(group, carry):
        for j in range(UNROLL):
            slot = entry * slots + group * UNROLL + j
            row, factor = cell[slot], weight[slot]
            tile, line = group * (UNROLL // 8) + j // 8, j % 8
            for k in range(2):
                out[k, tile, line : line + 1, :] = states[k][pl.ds(row, 1), :] * factor
        return carry

    lax.fori_loop(0, (count[entry] + UNROLL - 1) // UNROLL, pick, 0)


def own_kernel(size_z, size_x, place, cell, weight, count, first, second, out):
    slots = 8 * out.shape[2]

    def one(step, carry):
        out[step] = jnp.zeros(out.shape[1:], jnp.float32)
        receiver = receiver_of(step, place, size_z, size_x)
        pick_rows(out.at[step], receiver, slots, cell, weight, count, (first, second))
        return carry

    lax.fori_loop(0, out.shape[0], one, 0)


def bin_kernel(
    size_z, size_x, owned, place, cell, weight, count, station_own, station_pair, held, first, second, *rest
):
    out_a, out_b, picked = rest
    width = out_a.shape[3]
    cut = out_a.shape[2] - owned
    receivers, slots = station_own.shape
    order = lax.broadcasted_iota(jnp.int32, (1, slots), 1)
    picked[...] = jnp.zeros_like(picked)
    own = lax.broadcasted_iota(jnp.int32, (owned, slots), 0)

    def one(step, carry):
        receiver = receiver_of(step, place, size_z, size_x)
        pick_rows(picked, receivers + receiver, slots, cell, weight, count, (first, second))
        hots = []
        for e in range(2):
            station = (station_own, station_pair)[e][pl.ds(receiver, 1), :]
            live = order < count[e * receivers + receiver]
            hit = jnp.where(live, station, -1) == own
            hots.append(jnp.where(hit, 1.0, 0.0).astype(jnp.bfloat16))
        rows = [[held[step, k].reshape(slots, width) for k in range(2)]]
        rows.append([picked[k].reshape(slots, width) for k in range(2)])
        value = jnp.concatenate([jnp.concatenate(pair, axis=1) for pair in rows], axis=0)
        high = value.astype(jnp.bfloat16)
        low = (value - high.astype(jnp.float32)).astype(jnp.bfloat16)
        total = jnp.dot(
            jnp.concatenate(hots + hots, axis=1),
            jnp.concatenate([high, low], axis=0),
            preferred_element_type=jnp.float32,
        )
        ahead_z, ahead_x = step // size_x, step % size_x
        out_a[ahead_x, ahead_z, :owned, :] = total[:, :width]
        out_a[ahead_x, ahead_z, owned:, :] = total[:cut, width:]
        out_b[ahead_z, ahead_x] = total[cut:, width:]
        return carry

    lax.fori_loop(0, size_z * size_x, one, 0)


def bin_rows(place, cell, weight, count, station_own, station_pair, states, owned):
    size_z, size_x = lax.axis_size("z"), lax.axis_size("x")
    members, slots = states[0].shape[1], station_own.shape[1]
    rows_a = owned + owned // 4
    rows_b = 2 * owned - rows_a
    scalar = pl.BlockSpec(memory_space=pltpu.SMEM)
    whole = pl.BlockSpec(memory_space=pltpu.VMEM)
    held = pl.pallas_call(
        functools.partial(own_kernel, size_z, size_x),
        in_specs=[scalar] * 4 + [whole] * 2,
        out_specs=whole,
        out_shape=pltpu.VMEM((size_z * size_x, 2, slots // 8, 8, members), jnp.float32),
        compiler_params=pltpu.CompilerParams(vmem_limit_bytes=24 * 2**20),
        cost_estimate=pl.CostEstimate(
            flops=10**8, bytes_accessed=20 * 2**20, transcendentals=0
        ),
    )(place, cell, weight, count, *states[:2])
    return pl.pallas_call(
        functools.partial(bin_kernel, size_z, size_x, owned),
        in_specs=[scalar] * 4 + [whole] * 5,
        out_specs=[whole] * 2,
        out_shape=[
            pltpu.VMEM((size_x, size_z, rows_a, members), jnp.float32),
            pltpu.VMEM((size_z, size_x, rows_b, members), jnp.float32),
        ],
        scratch_shapes=[pltpu.VMEM((2, slots // 8, 8, members), jnp.float32)],
        compiler_params=pltpu.CompilerParams(vmem_limit_bytes=32 * 2**20),
        cost_estimate=pl.CostEstimate(flops=10**9, bytes_accessed=30 * 2**20, transcendentals=0),
    )(place, cell, weight, count, station_own, station_pair, held, *states[2:])


def factor_kernel(root_scale, products, high, low):
    size = products.shape[1]
    lane = lax.broadcasted_iota(jnp.int32, (size, size), 1)
    line = lax.broadcasted_iota(jnp.int32, (size, size), 0)
    eye = jnp.where(lane == line, 1.0, 0.0)
    left, right = products[:size, :] + eye, eye
    width = 4
    done_left, done_right = [], []
    for start in range(0, size, width):
        top = start % 8
        columns = [
            jnp.broadcast_to(left[:, start + a : start + a + 1], left.shape) for a in range(width)
        ]
        pivots = [[columns[b][top + a : top + a + 1, :] for b in range(width)] for a in range(width)]
        upper = [[None] * width for _ in range(width)]
        inverse = []
        for a in range(width):
            lower = []
            for k in range(a):
                value = pivots[a][k]
                for m in range(k):
                    value = value - lower[m] * upper[m][k]
                lower.append(value * inverse[k])
            for b in range(a, width):
                value = pivots[a][b]
                for m in range(a):
                    value = value - lower[m] * upper[m][b]
                upper[a][b] = value
            inverse.append(1.0 / upper[a][a])
        below = line[: left.shape[0]]
        multipliers = []
        for a in range(width):
            value = columns[a]
            for m in range(a):
                value = value - multipliers[m] * upper[m][a]
            value = value * inverse[a]
            multipliers.append(jnp.where(below > top + a, value, 0.0))
        rows_left, rows_right = [], []
        for a in range(width):
            row_left = left[top + a : top + a + 1, :]
            row_right = right[top + a : top + a + 1, :]
            for m in range(a):
                scale = multipliers[m][top + a : top + a + 1, :]
                row_left = row_left - scale * rows_left[m]
                row_right = row_right - scale * rows_right[m]
            rows_left.append(row_left)
            rows_right.append(row_right)
        for m in range(width):
            left = left - multipliers[m] * rows_left[m]
            right = right - multipliers[m] * rows_right[m]
        if top + width == 8:
            done_left.append(left[:8])
            done_right.append(right[:8])
            left, right = left[8:], right[8:]
    left = jnp.concatenate(done_left, axis=0)
    right = jnp.concatenate(done_right, axis=0)
    pivot = jnp.sum(jnp.where(lane == line, left, 0.0), axis=1, keepdims=True)
    inverse = right * lax.rsqrt(pivot)
    push = products[size : size + 1, :]
    pushed = jnp.sum(inverse * push, axis=1, keepdims=True)
    offset = jnp.sum(inverse * pushed, axis=0, keepdims=True) * (1.0 / root_scale)
    weights = inverse + offset
    weights = weights - jnp.mean(weights, axis=1, keepdims=True) + 1.0 / size
    top_half = weights.astype(jnp.bfloat16)
    high[...] = top_half
    low[...] = (weights - top_half.astype(jnp.float32)).astype(jnp.bfloat16)


def transposed_weights(products, root_scale):
    size = products.shape[1]
    whole = pl.BlockSpec(memory_space=pltpu.VMEM)
    return pl.pallas_call(
        functools.partial(factor_kernel, root_scale),
        in_specs=[whole],
        out_specs=[whole] * 2,
        out_shape=[pltpu.VMEM((size, size), jnp.bfloat16)] * 2,
    )(products)


def analysis_kernel(high, low, state, observed, out, out_observed):
    def update(value):
        near = value.astype(jnp.bfloat16)
        rest = (value - near.astype(jnp.float32)).astype(jnp.bfloat16)

        def times(a, b):
            return lax.dot_general(
                a, b[...], (((1,), (1,)), ((), ())), preferred_element_type=jnp.float32
            )

        return times(near, high) + (times(rest, high) + times(near, low))

    out[...] = update(state[...])

    @pl.when(pl.program_id(0) == 0)
    def _():
        out_observed[...] = update(observed[...])


def analyse(high, low, state, observed):
    rows, members = state.shape
    whole = pl.BlockSpec(memory_space=pltpu.VMEM)
    block = pl.BlockSpec((rows // 8, members), lambda k: (k, 0))
    return pl.pallas_call(
        analysis_kernel,
        grid=(8,),
        in_specs=[whole, whole, block, whole],
        out_specs=[block, pl.BlockSpec(observed.shape, lambda k: (0, 0))],
        out_shape=[
            jax.ShapeDtypeStruct(state.shape, jnp.float32),
            jax.ShapeDtypeStruct(observed.shape, jnp.float32),
        ],
    )(high, low, state, observed)


def ring_reduce(blocks, axis):
    count = len(blocks)
    half = count // 2
    cut = blocks[half].shape[-2] // 2
    up = shift(blocks[half][..., :cut, :], axis, 1)
    down = shift(blocks[half][..., cut:, :], axis, -1)
    ahead, behind = blocks[half - 1], blocks[count - half + 1]
    up = jnp.concatenate([ahead[..., :cut, :] + up, ahead[..., cut:, :]], axis=-2)
    down = jnp.concatenate([behind[..., :cut, :], behind[..., cut:, :] + down], axis=-2)
    for k in range(half - 1, 0, -1):
        up = shift(up, axis, 1)
        down = shift(down, axis, -1)
        if k > 1:
            up = blocks[k - 1] + up
            down = blocks[count - k + 1] + down
    return blocks[0] + up + down


def reduce_to_owner(block_a, block_b):
    size_x, size_z = block_a.shape[:2]
    part_a = ring_reduce([block_a[k] for k in range(size_x)], "x")
    part_b = ring_reduce([block_b[k] for k in range(size_z)], "z")
    part_a = ring_reduce([part_a[k] for k in range(size_z)], "z")
    part_b = ring_reduce([part_b[k] for k in range(size_x)], "x")
    return jnp.concatenate([part_a, part_b], axis=0)


def spread_sum(value, axis):
    count = math.prod(lax.axis_size(name) for name in axis)
    copies = jnp.broadcast_to(value[None], (count,) + value.shape)
    return jnp.sum(lax.all_to_all(copies, axis, split_axis=0, concat_axis=0, tiled=True), axis=0)


def sum_everywhere(value):
    core = lax.axis_index("core")
    rows = value.shape[0] // 2
    value = value + shift(value, "core", 1)
    part = lax.dynamic_slice_in_dim(value, core * rows, rows, 0)
    for axis in (("lat", "x"), ("z",)):
        part = spread_sum(part, axis)
    other = shift(part, "core", 1)
    return jnp.where(
        core == 0, jnp.concatenate([part, other]), jnp.concatenate([other, part])
    )


def on_device(
    control,
    perturbations,
    zonal_flow,
    meridional_flow,
    diffusivity,
    send_cell,
    send_station,
    send_weight,
    send_count,
    obs_value,
    obs_error,
):
    member_count = perturbations.shape[2]
    step_total, owned_count = obs_value.shape
    place = jnp.stack([lax.axis_index(name) for name in COL]).astype(jnp.int32)
    swapped = [
        shift(table[0, 0], "core", 1)
        for table in (send_cell, send_weight, send_count, send_station)
    ]

    zero = jnp.zeros_like(control)
    rates = jnp.stack(
        [
            diffusivity + jnp.maximum(-zonal_flow, 0.0),
            diffusivity + jnp.maximum(zonal_flow, 0.0),
            diffusivity + jnp.maximum(-meridional_flow, 0.0),
            diffusivity + jnp.maximum(meridional_flow, 0.0),
            control,
            zero,
            zero,
            zero,
        ],
        axis=1,
    ).reshape(-1, member_count, control.shape[1])
    first = advance(True, rates, perturbations, edges(ends_of(perturbations, control)))
    tables = [
        jnp.concatenate([table[0, 0], other], axis=0).reshape(-1)
        for table, other in zip((send_cell, send_weight, send_count), swapped)
    ] + [send_station[0, 0], swapped[3]]
    sides, tables = lax.optimization_barrier((edges(ends_of(first)), tables))
    second = advance(False, rates, first, sides)
    flat = [state.reshape(-1, member_count) for state in (first, second)]
    paired = [shift(state, "core", 1) for state in flat]
    blocks = bin_rows(place, *tables, flat + paired, owned_count)
    observed = reduce_to_owner(*blocks).reshape(step_total, owned_count, member_count)

    root_scale = math.sqrt(member_count - 1.0)
    obs_mean = jnp.mean(observed, axis=2)
    spread = observed - obs_mean[:, :, None]
    scaled = (spread / (obs_error[:, :, None] * root_scale)).reshape(-1, member_count)
    innovation = ((obs_value - obs_mean) / obs_error).reshape(-1)
    products = jnp.dot(
        jnp.concatenate(
            [scaled, innovation[:, None], jnp.zeros((scaled.shape[0], 15), jnp.float32)], axis=1
        ).T,
        scaled,
        precision=exact_mode,
    )
    products = sum_everywhere(products)
    high, low = transposed_weights(products, root_scale)
    analysis, obs_analysis = analyse(
        high, low, flat[-1], observed.reshape(-1, member_count)
    )
    return (analysis.reshape(perturbations.shape), obs_analysis.reshape(observed.shape))


def solution(mesh):
    sizes = (mesh.shape["lat"], mesh.shape["col"] // 8, 4, 2)
    fine = Mesh(mesh.devices.reshape(sizes), ("lat",) + COL)
    grid = P("lat", COL)
    return jax.shard_map(
        on_device,
        mesh=fine,
        in_specs=(
            grid,
            P("lat", COL, None),
            grid,
            grid,
            grid,
            P("lat", COL, None, None),
            P("lat", COL, None, None),
            P("lat", COL, None, None),
            P("lat", COL, None),
            P(None, ("lat",) + COL),
            P(None, ("lat",) + COL),
        ),
        out_specs=(P("lat", COL, None), P(None, ("lat",) + COL, None)),
        check_vma=False,
    )
```
